512 devices in a mesh: orb: 32 (over x, y, core), pln: 16 (over z).
Axes of the slice: x: 4, y: 4, z: 16, core: 2. Of those that a mesh axis runs over, the one named last changes fastest.
Arguments:
- orbitals: bfloat16 [512, 32768], P('orb'), may hold values from -6 to 6
- occupations: float32 [512], P('orb'), may hold values from 0.5 to 2
- box_offsets: int32 [512, 3], P('orb'), may hold values from 0 to 96
- kernel_spectrum: float32 [256, 256, 256], P(None, 'pln', 'orb'), may hold values from 0.05 to 3.4, as said below
Outputs:
- hartree_terms: bfloat16 [512, 32768], P('orb', 'pln')
The draws below stay inside these ranges and needn't reach their ends.
Inputs may be any that keep to these rules, and one draw needn't show every extreme that they name: `box_offsets`: each orbital's box of 32 cells a side lies inside the fine grid. `kernel_spectrum`: positive and even: unchanged when any index k is replaced by (256 - k) mod 256.
All inputs are finite; a program needn't handle non-finite values.
Results may differ from the reference program's by a relative error of at most 0.003.
Values may be sent and summed in bfloat16 or wider, within the bound.
A program may use at most 128 MiB of HBM per device.

```python
import math
import jax
import jax.numpy as jnp
from jax import lax

G = 128
BOX = 32
NORB = 512
M = 256
BOX3 = 32768


def draw_kernel_spectrum(key, part):
    half = M // 2 + 1
    steps = jnp.arange(M, dtype=jnp.int32)
    folded = jnp.minimum(steps, M - steps)
    rough = jnp.exp(jax.random.uniform(key, (half, half, half), jnp.float32, math.log(0.5), math.log(2.0)))
    strength = 8.0
    squares = (folded[:, None, None] ** 2 + folded[None, :, None] ** 2 + folded[None, None, :] ** 2).astype(jnp.float32)
    table = rough[folded[:, None, None], folded[None, :, None], folded[None, None, :]]
    return (0.1 * table * (1.0 + strength / (1.0 + squares / 4.0))).astype(jnp.float32)


def with_ends(entries, own_key, low, largest):
    spot = [jax.random.randint(jax.random.fold_in(own_key, axis), (), 0, length) for axis, length in enumerate(entries.shape)]
    widest = entries.shape.index(max(entries.shape))
    neighbour = spot[:widest] + [(spot[widest] + 1) % entries.shape[widest]] + spot[widest + 1:]
    return entries.at[tuple(spot)].set(low).at[tuple(neighbour)].set(largest)


def block_levels(key, shape, split, least, high):
    gain, own = 1.0, jax.random.fold_in(key, 6)
    for dim, shards_of in split:
        steps = jnp.exp(jax.random.uniform(jax.random.fold_in(own, dim), (shards_of,), jnp.float32, least / len(split), high / len(split)))
        gain = gain * jnp.repeat(steps, shape[dim] // shards_of).reshape([-1 if axis == dim else 1 for axis in range(len(shape))])
    return gain


def centred(rng, dims, scale, most, pieces=(), kind=jnp.bfloat16):
    factor_of = block_levels(rng, dims, pieces, -0.22, 0.18) if pieces else 1.0
    result = jax.random.normal(rng, dims, jnp.float32) * scale * factor_of
    return jnp.minimum(jnp.maximum(result, -most), most).astype(kind)


def setup_inputs(seed: int = 0) -> dict:
    streams_of = jax.random.split(jax.random.key(seed), 5)
    orbitals = centred(streams_of[0], (NORB, BOX3), 1.0, 6.0, ((0, 32),))
    occupations = jnp.clip(0.5 + 1.5 * jax.random.uniform(streams_of[1], (NORB,), jnp.float32) ** block_levels(streams_of[1], (NORB,), ((0, 32),), -0.2, 0.2), 0.5, 2.0)
    box_offsets = with_ends(jax.random.randint(streams_of[2], (NORB, 3), 0, G - BOX + 1), jax.random.fold_in(streams_of[2], 1), 0, G - BOX).astype(jnp.int32)
    kernel_spectrum = draw_kernel_spectrum(jax.random.fold_in(streams_of[4], 71), 0)
    return dict(orbitals=orbitals, occupations=occupations, box_offsets=box_offsets, kernel_spectrum=kernel_spectrum)


MAGIC_TAPS = (8.4334247333529341e-7, -1.2905572013420610e-5, 8.7629844762105596e-5, -3.0158038132690463e-4, 1.7472371367299390e-3, -9.4204703020108039e-3, 2.3738214637249424e-2, 6.1262589583120798e-2, 9.9404156978340040e-1, -6.0489528919698352e-2, -2.1030251609303814e-2, 1.3372634148547948e-2, -3.4412814449349386e-3, 4.9443227688689919e-4, -5.1859868811734329e-5, 2.7273449291197966e-6)
PRECISE = lax.Precision.HIGHEST


def magic_matrix(positions, width):
    taps = jnp.array(MAGIC_TAPS, dtype=jnp.float32)
    shifted = jnp.arange(width, dtype=jnp.int32)[None, :] - positions[:, None]
    hits = (shifted[:, :, None] == jnp.arange(-8, 8, dtype=jnp.int32)[None, None, :]).astype(jnp.float32)
    inside = ((positions >= 0) & (positions < width)).astype(jnp.float32)
    return jnp.sum(hits * taps, axis=2) * inside[:, None]


def expand(coef, filters):
    section = jnp.einsum('jk,kyx->jyx', filters, coef, precision=PRECISE)
    section = jnp.einsum('ak,jkx->jax', filters, section, precision=PRECISE)
    return jnp.einsum('bx,jax->jab', filters, section, precision=PRECISE)


def contract(weighted, filters):
    section = jnp.einsum('bx,jab->jax', filters, weighted, precision=PRECISE)
    section = jnp.einsum('ak,jax->jkx', filters, section, precision=PRECISE)
    return jnp.einsum('jk,jyx->kyx', filters, section, precision=PRECISE)


def reference(orbitals, occupations, box_offsets, kernel_spectrum):
    filters = magic_matrix(jnp.arange(BOX, dtype=jnp.int32), BOX)
    coefs = orbitals.astype(jnp.float32).reshape(NORB, BOX, BOX, BOX)

    def add_one(grid, item):
        coef, weight, corner = item
        psi = expand(coef, filters)
        where = (corner[0], corner[1], corner[2])
        current = lax.dynamic_slice(grid, where, (BOX, BOX, BOX))
        return lax.dynamic_update_slice(grid, current + weight * psi * psi, where), None

    density, _ = lax.scan(add_one, jnp.zeros((G, G, G), jnp.float32), (coefs, occupations, box_offsets.astype(jnp.int32)))
    padded = jnp.pad(density, ((0, G), (0, G), (0, G)))
    spectrum = jnp.fft.fftn(padded) * kernel_spectrum
    potential = jnp.real(jnp.fft.ifftn(spectrum))[:G, :G, :G].astype(jnp.float32)

    def apply_one(item):
        coef, corner = item
        psi = expand(coef, filters)
        local = lax.dynamic_slice(potential, (corner[0], corner[1], corner[2]), (BOX, BOX, BOX))
        return contract(local * psi, filters).reshape(BOX * BOX * BOX)

    terms = lax.map(apply_one, (coefs, box_offsets.astype(jnp.int32)))
    return terms.astype(jnp.bfloat16)
```

```python
import math

import jax
import jax.numpy as jnp
import numpy as np
from jax import lax
from jax.experimental import pallas as pl
from jax.experimental.pallas import tpu as pltpu
from jax.sharding import PartitionSpec as P

G = 128
BOX = 32
M = 256
N_ORB = 32
N_PLN = 16
BF = jnp.bfloat16
F32 = jnp.float32

MAGIC_TAPS = (
    8.433424733352934e-07,
    -1.290557201342061e-05,
    8.76298447621056e-05,
    -0.00030158038132690465,
    0.001747237136729939,
    -0.009420470302010804,
    0.023738214637249424,
    0.0612625895831208,
    0.9940415697834004,
    -0.06048952891969835,
    -0.021030251609303816,
    0.013372634148547948,
    -0.0034412814449349387,
    0.0004944322768868992,
    -5.185986881173433e-05,
    2.7273449291197967e-06,
)


def split(values):
    high = np.asarray(values, np.float32).astype(BF)
    low = (np.asarray(values, np.float32) - high.astype(np.float32)).astype(BF)
    return np.stack([high, low])


def tables():
    taps = np.asarray(MAGIC_TAPS, np.float32)
    magic = np.zeros((BOX, BOX), np.float32)
    for i in range(BOX):
        for k in range(BOX):
            if -8 <= k - i <= 7:
                magic[i, k] = taps[k - i + 8]
    depth = np.zeros((G, BOX * N_PLN), np.float32)
    depth[32 : 32 + BOX] = np.repeat(magic, N_PLN, axis=1)
    angle = 2.0 * math.pi * (np.outer(np.arange(M), np.arange(G)) % M) / M
    hartley = np.cos(angle) + np.sin(angle)
    inner = np.tile(magic.T, (1, BOX)).astype(np.float32)
    outer = np.repeat(magic.T, BOX, axis=1).astype(np.float32)
    back = np.concatenate([magic[:, 0::2].T, magic[:, 1::2].T])
    return split(depth), split(hartley), split(hartley.T), inner, outer, split(back), float(magic[0, 0]) ** 2


def dg(a, b, ca, cb):
    return lax.dot_general(a, b, (((ca,), (cb,)), ((), ())), preferred_element_type=F32)


def halves(a):
    high = a.astype(BF)
    return high, (a - high.astype(F32)).astype(BF)


def dot3(a, bh, bl, ca, cb):
    ah, al = halves(a)
    return dg(ah, bh, ca, cb) + (dg(al, bh, ca, cb) + dg(ah, bl, ca, cb))


def dot3r(ah, al, b, ca, cb):
    bh, bl = halves(b)
    return dg(ah, bh, ca, cb) + (dg(al, bh, ca, cb) + dg(ah, bl, ca, cb))


def kernel(
    main,
    orb_ref, occ_ref, off_ref, ker_ref, depth_ref, har_ref, hart_ref, inner_ref, outer_ref, back_ref,
    out_ref,
    x_s, kt_s, psq_s, own_s, q_s, d_s, s1, r1, tr_s, s2, r2, s3, r3, w_s, r4, s5, r5, fs_s, s6, r6, gs_s, kp_s,
    send_sem, rs1, rs2, rs3, rs4, rs5, rs6,
):
    o = lax.axis_index("orb")
    p = lax.axis_index("pln")
    barrier = pltpu.get_barrier_semaphore()

    def greet(axis, me, count):
        def step(d, carry):
            pl.semaphore_signal(
                barrier, inc=1, device_id={axis: lax.rem(me + d, count)}, device_id_type=pl.DeviceIdType.MESH
            )
            return carry

        lax.fori_loop(1, count, step, 0)

    greet("orb", o, N_ORB)
    greet("pln", p, N_PLN)

    def copy_to(axis, src, dst, recv, slot, other, sem_slot):
        return pltpu.make_async_remote_copy(
            src_ref=src, dst_ref=dst, send_sem=send_sem.at[sem_slot], recv_sem=recv.at[slot],
            device_id={axis: other}, device_id_type=pl.DeviceIdType.MESH,
        )

    def send_all(axis, me, count, src_of, dst, recv):
        def step(d, carry):
            other = lax.rem(me + d, count)
            copy_to(axis, src_of(other), dst.at[me], recv, me, other, d).start()
            return carry

        lax.fori_loop(1, count, step, 0)

    def wait_all(axis, me, count, src_of, dst, recv, each=None):
        def step(d, carry):
            other = lax.rem(me + d, count)
            copy_to(axis, src_of(other), dst.at[other], recv, other, other, d).wait()
            return carry

        lax.fori_loop(1, count, step, 0)

    for k in range(BOX):
        x_s[k * 16 : (k + 1) * 16, :] = orb_ref[:, k * 1024 : (k + 1) * 1024]
    col1024 = lax.broadcasted_iota(jnp.int32, (BOX, 1024), 1)
    row32 = lax.broadcasted_iota(jnp.int32, (BOX, 1024), 0)
    inner = inner_ref[...]

    def make_kt(q, carry):
        block = inner * outer_ref[pl.ds(q, 1), :]
        block = jnp.where(col1024 == row32 + q * BOX, 0.0, block)
        kt_s[pl.ds(pl.multiple_of(q * BOX, BOX), BOX), :] = block.astype(BF)
        return carry

    lax.fori_loop(0, BOX, make_kt, 0)

    lane = lax.broadcasted_iota(jnp.int32, (8, 128), 1)
    row8 = lax.broadcasted_iota(jnp.int32, (8, 128), 0)
    hot = jnp.concatenate(
        [jnp.where(lane == row8 + (8 * p - off_ref[n, 0] + 32), 1.0, 0.0) for n in range(N_PLN)], axis=0
    ).astype(BF)
    same = (
        lax.broadcasted_iota(jnp.int32, (128, 512), 0) // 8 == lax.broadcasted_iota(jnp.int32, (128, 512), 1) % N_PLN
    )
    eh = jnp.where(same, dg(hot, depth_ref[0], 1, 0), 0.0).astype(BF)
    el = jnp.where(same, dg(hot, depth_ref[1], 1, 0), 0.0).astype(BF)
    x = x_s[...]
    s = dg(eh, x, 1, 0) + dg(el, x, 1, 0)
    psi = main * s + dg(s.astype(BF), kt_s[...], 1, 0)
    psq_s[...] = psi * psi


    def place(n, carry):
        weight = occ_ref[n]
        ox = off_ref[n, 2]
        inside = (lane >= ox) & (lane < ox + BOX)
        for bt in range(8):
            v = psq_s[pl.ds(pl.multiple_of(n * 8, 8), 8), bt * 128 : (bt + 1) * 128] * weight
            for j in range(4):
                turned = pltpu.roll(v, lax.rem(ox + 128 - 32 * j, 128), 1)
                at = pl.multiple_of((n * BOX + bt * 4 + j) * 8, 8)
                q_s[pl.ds(at, 8), :] = jnp.where(inside, turned, 0.0)
        return carry

    lax.fori_loop(0, N_PLN, place, 0)

    lane_n = lax.broadcasted_iota(jnp.int32, (1, 512), 1)
    oy = jnp.zeros((1, 512), jnp.int32)
    for n in range(N_PLN):
        oy = jnp.where(lane_n // BOX == n, off_ref[n, 1], oy)
    target = oy + lane_n % BOX
    spots = jnp.where(lax.broadcasted_iota(jnp.int32, (G, 512), 0) == target, 1.0, 0.0).astype(BF)
    hh, hl = har_ref[0], har_ref[1]

    def plane(z, carry):
        qz = q_s[pl.ds(z, 512, stride=8), :]
        qh, ql = halves(qz)
        a = dg(spots, qh, 1, 0) + dg(spots, ql, 1, 0)
        d_s[pl.ds(z, 256, stride=8), :] = dot3r(hh, hl, a, 1, 1)
        return carry

    lax.fori_loop(0, 8, plane, 0)
    s1[...] = d_s[...].reshape(N_ORB, 64, 128).astype(BF)

    pl.semaphore_wait(barrier, N_ORB - 1 + N_PLN - 1)
    send_all("orb", o, N_ORB, lambda i: s1.at[i], r1, rs1)

    lane_own = lax.broadcasted_iota(jnp.int32, (BOX, 512), 1) % N_PLN
    oh = jnp.where(lane_own == p, depth_ref[0, 32 : 32 + BOX, :].astype(F32), 0.0).astype(BF)
    ol = jnp.where(lane_own == p, depth_ref[1, 32 : 32 + BOX, :].astype(F32), 0.0).astype(BF)
    s_own = dg(oh, x_s[...], 1, 0) + dg(ol, x_s[...], 1, 0)
    own_s[...] = main * s_own + dg(s_own.astype(BF), kt_s[...], 1, 0)

    for h in range(2):
        d_s[h * 128 : (h + 1) * 128, :] = ker_ref[:, h * 128 : (h + 1) * 128] * (1.0 / float(M) ** 3)
    for kx in range(8):
        for h in range(2):
            kp_s[kx * 16 : (kx + 1) * 16, h * 128 : (h + 1) * 128] = d_s[pl.ds(h * 128 + kx, 16, stride=8), :]

    wait_all("orb", o, N_ORB, lambda i: s1.at[i], r1, rs1)

    def add(d, total):
        return total + r1[lax.rem(o + d, N_ORB)].astype(F32)

    tr = lax.fori_loop(1, N_ORB, add, s1[o].astype(F32))

    y = dot3(tr, hh, hl, 1, 1)
    for i in range(N_PLN):
        total = jnp.zeros((8, 128), F32)
        for kx in range(8):
            v = y[kx * 8 : (kx + 1) * 8, (i // 8) * 128 : (i // 8) * 128 + 128]
            shift = 16 * (kx - i % 8) % 128
            v = pltpu.roll(v, shift, 1) if shift else v
            total = jnp.where(lane // 16 == kx, v, total)
        s2[i] = total
    send_all("pln", p, N_PLN, lambda i: s2.at[i], r2, rs2)
    r2[p] = s2[p]
    wait_all("pln", p, N_PLN, lambda i: s2.at[i], r2, rs2)

    grid_z = r2[...].reshape(G, 128)
    spectrum = dot3(grid_z.T, hh, hl, 1, 1)
    spectrum = spectrum * kp_s[...]
    back_z = dot3r(hart_ref[0], hart_ref[1], spectrum, 1, 1)
    s3[...] = back_z.reshape(N_PLN, 8, 128)
    send_all("pln", p, N_PLN, lambda i: s3.at[i], r3, rs3)
    r3[p] = s3[p]
    wait_all("pln", p, N_PLN, lambda i: s3.at[i], r3, rs3)

    blocks = []
    for kx in range(8):
        sides = []
        for h in range(2):
            total = jnp.zeros((8, 128), F32)
            for i in range(8):
                v = r3[h * 8 + i]
                shift = 16 * (i - kx) % 128
                v = pltpu.roll(v, shift, 1) if shift else v
                total = jnp.where(lane // 16 == i, v, total)
            sides.append(total)
        blocks.append(jnp.concatenate(sides, axis=1))
    w_s[...] = dot3(jnp.concatenate(blocks, axis=0), hh, hl, 1, 0)
    send_all("orb", o, N_ORB, lambda i: w_s, r4, rs4)
    r4[o] = w_s[...]
    wait_all("orb", o, N_ORB, lambda i: w_s, r4, rs4)

    d_s[...] = r4[...].reshape(N_ORB * 64, 128)

    def plane_back(z, carry):
        wz = d_s[pl.ds(z, 256, stride=8), :]
        vh, vl = halves(dot3(wz.T, hh, hl, 1, 0))
        q_s[pl.ds(z, 512, stride=8), :] = dg(spots, vh, 0, 0) + dg(spots, vl, 0, 0)
        return carry

    lax.fori_loop(0, 8, plane_back, 0)

    def box(n, carry):
        ox = off_ref[n, 2]
        for bt in range(8):
            total = jnp.zeros((8, 128), F32)
            for j in range(4):
                v = q_s[pl.ds(pl.multiple_of((n * BOX + bt * 4 + j) * 8, 8), 8), :]
                v = pltpu.roll(v, lax.rem(128 + 32 * j - ox, 128), 1)
                total = jnp.where(lane // 32 == j, v, total)
            s5[n, :, bt * 128 : (bt + 1) * 128] = total
        return carry

    lax.fori_loop(0, N_PLN, box, 0)
    send_all("pln", p, N_PLN, lambda i: s5.at[i], r5, rs5)
    r5[p] = s5[p]
    wait_all("pln", p, N_PLN, lambda i: s5.at[i], r5, rs5)

    bh, bl = halves(r5[...].reshape(G, 1024))
    cut = jnp.where(
        lax.broadcasted_iota(jnp.int32, (BOX, G), 1) == lax.broadcasted_iota(jnp.int32, (BOX, G), 0) + off_ref[p, 0], 1.0, 0.0
    ).astype(BF)
    v_box = dg(cut, bh, 1, 0) + dg(cut, bl, 1, 0)
    u = v_box * own_s[...]
    u = main * u + dg(u.astype(BF), kt_s[...], 1, 1)
    f = dot3r(back_ref[0], back_ref[1], u, 1, 0)
    for t in range(16):
        part = f[(t // 8) * 16 : (t // 8) * 16 + 16, (t % 8) * 128 : (t % 8) * 128 + 128]
        fs_s[t * 16 : (t + 1) * 16, :] = part
    for i in range(N_PLN):
        s6[i] = fs_s[pl.ds(i, 16, stride=16), :].astype(BF)
    send_all("pln", p, N_PLN, lambda i: s6.at[i], r6, rs6)
    r6[p] = s6[p]
    wait_all("pln", p, N_PLN, lambda i: s6.at[i], r6, rs6)
    gs_s[...] = r6[...].astype(F32).reshape(256, 128)
    for t in range(16):
        out_ref[:, t * 128 : (t + 1) * 128] = gs_s[pl.ds(t, 16, stride=16), :].astype(BF)


def per_device(orbitals, occupations, box_offsets, kernel_spectrum):
    depth, har, hart, inner, outer, back, main = tables()
    ker = kernel_spectrum.transpose(1, 2, 0).reshape(128, M)
    vm = pl.BlockSpec(memory_space=pltpu.VMEM)
    sm = pl.BlockSpec(memory_space=pltpu.SMEM)
    V = pltpu.VMEM
    dma = pltpu.SemaphoreType.DMA

    def body(*refs):
        kernel(main, *refs)

    return pl.pallas_call(
        body,
        out_shape=jax.ShapeDtypeStruct((16, 2048), BF),
        in_specs=[vm, sm, sm] + [vm] * 7,
        out_specs=vm,
        scratch_shapes=[
            V((512, 1024), BF),
            V((1024, 1024), BF),
            V((128, 1024), F32),
            V((32, 1024), F32),
            V((4096, 128), F32),
            V((2048, 128), F32),
            V((32, 64, 128), BF),
            V((32, 64, 128), BF),
            V((64, 128), F32),
            V((16, 8, 128), F32),
            V((16, 8, 128), F32),
            V((16, 8, 128), F32),
            V((16, 8, 128), F32),
            V((64, 128), F32),
            V((32, 64, 128), F32),
            V((16, 8, 1024), F32),
            V((16, 8, 1024), F32),
            V((256, 128), F32),
            V((16, 16, 128), BF),
            V((16, 16, 128), BF),
            V((256, 128), F32),
            V((128, 256), F32),
            dma((32,)), dma((32,)), dma((16,)), dma((16,)), dma((32,)), dma((16,)), dma((16,)),
        ],
        compiler_params=pltpu.CompilerParams(collective_id=0, has_side_effects=True, vmem_limit_bytes=48 << 20),
        name="hartree",
    )(orbitals, occupations, box_offsets, ker, depth, har, hart, inner, outer, back)


def solution(mesh):
    in_specs = (P("orb", None), P("orb"), P("orb", None), P(None, "pln", "orb"))
    out_specs = P("orb", "pln")
    return jax.shard_map(per_device, mesh=mesh, in_specs=in_specs, out_specs=out_specs, check_vma=False)
```

```python
import math

import jax
import jax.numpy as jnp
import numpy as np
from jax import lax
from jax.experimental import pallas as pl
from jax.experimental.pallas import tpu as pltpu
from jax.sharding import PartitionSpec as P

G = 128
BOX = 32
M = 256
N_ORB = 32
N_PLN = 16
BF = jnp.bfloat16
F32 = jnp.float32

MAGIC_TAPS = (
    8.433424733352934e-07,
    -1.290557201342061e-05,
    8.76298447621056e-05,
    -0.00030158038132690465,
    0.001747237136729939,
    -0.009420470302010804,
    0.023738214637249424,
    0.0612625895831208,
    0.9940415697834004,
    -0.06048952891969835,
    -0.021030251609303816,
    0.013372634148547948,
    -0.0034412814449349387,
    0.0004944322768868992,
    -5.185986881173433e-05,
    2.7273449291197967e-06,
)


NEAR = sorted(
    [(a, b) for a in range(4) for b in range(4) if (a, b) != (0, 0)],
    key=lambda d: min(d[0], 4 - d[0]) + min(d[1], 4 - d[1]),
)


def split(values):
    high = np.asarray(values, np.float32).astype(BF)
    low = (np.asarray(values, np.float32) - high.astype(np.float32)).astype(BF)
    return np.stack([high, low])


def tables():
    taps = np.asarray(MAGIC_TAPS, np.float32)
    magic = np.zeros((BOX, BOX), np.float32)
    for i in range(BOX):
        for k in range(BOX):
            if -8 <= k - i <= 7:
                magic[i, k] = taps[k - i + 8]
    depth = np.zeros((G, BOX * N_PLN), np.float32)
    depth[32 : 32 + BOX] = np.repeat(magic, N_PLN, axis=1)
    angle = 2.0 * math.pi * (np.outer(np.arange(M), np.arange(G)) % M) / M
    hartley = np.cos(angle) + np.sin(angle)
    inner = np.tile(magic.T, (1, BOX)).astype(np.float32)
    outer = np.repeat(magic.T, BOX, axis=1).astype(np.float32)
    back = np.concatenate([magic[:, 0::2].T, magic[:, 1::2].T])
    return split(depth), split(hartley), split(hartley.T), inner, outer, split(back), float(magic[0, 0]) ** 2


def dg(a, b, ca, cb):
    return lax.dot_general(a, b, (((ca,), (cb,)), ((), ())), preferred_element_type=F32)


def halves(a):
    high = a.astype(BF)
    return high, (a - high.astype(F32)).astype(BF)


def dot3(a, bh, bl, ca, cb):
    ah, al = halves(a)
    return dg(ah, bh, ca, cb) + (dg(al, bh, ca, cb) + dg(ah, bl, ca, cb))


def dot3r(ah, al, b, ca, cb):
    bh, bl = halves(b)
    return dg(ah, bh, ca, cb) + (dg(al, bh, ca, cb) + dg(ah, bl, ca, cb))


def kernel(
    main,
    orb_hbm, occ_ref, off_ref, ker_hbm, depth_hbm, har_hbm, hart_hbm, inner_hbm, outer_hbm, back_hbm,
    out_ref,
    ker_ref, depth_ref, har_ref, hart_ref, inner_ref, outer_ref, back_ref,
    x_s, kt_s, psq_s, own_s, q_s, d_s, s1, r1, tr_s, s2, r2, s3, r3, w_s, r4, s5, r5, fs_s, s6, r6, gs_s, kp_s,
    load_sem, send_sem, rs1, rs2, rs3, rs4, rs5, rs6,
):
    o = lax.axis_index("orb")
    p = lax.axis_index("pln")
    barrier = pltpu.get_barrier_semaphore()

    def greet(axis, me, count):
        def step(d, carry):
            pl.semaphore_signal(
                barrier, inc=1, device_id={axis: lax.rem(me + d, count)}, device_id_type=pl.DeviceIdType.MESH
            )
            return carry

        lax.fori_loop(1, count, step, 0)

    greet("orb", o, N_ORB)
    greet("pln", p, N_PLN)

    pairs = (
        (depth_hbm, depth_ref), (inner_hbm, inner_ref), (outer_hbm, outer_ref), (har_hbm, har_ref),
        (ker_hbm, ker_ref), (hart_hbm, hart_ref), (back_hbm, back_ref),
    )
    loads = [pltpu.make_async_copy(a, b, load_sem.at[i]) for i, (a, b) in enumerate(pairs)]
    rows_of = lambda k: pltpu.make_async_copy(
        orb_hbm.at[:, pl.ds(pl.multiple_of(k * 1024, 1024), 1024)],
        x_s.at[pl.ds(pl.multiple_of(k * 16, 16), 16), :],
        load_sem.at[8 + k],
    )

    def start_rows(k, carry):
        rows_of(k).start()
        return carry

    def wait_rows(k, carry):
        rows_of(k).wait()
        return carry

    for i in (1, 2, 0):
        loads[i].start()
    lax.fori_loop(0, BOX, start_rows, 0)
    for i in (3, 4, 5, 6):
        loads[i].start()
    loads[1].wait()
    loads[2].wait()

    def copy_to(axis, src, dst, recv, slot, other, sem_slot):
        return pltpu.make_async_remote_copy(
            src_ref=src, dst_ref=dst, send_sem=send_sem.at[sem_slot], recv_sem=recv.at[slot],
            device_id={axis: other}, device_id_type=pl.DeviceIdType.MESH,
        )

    def send_all(axis, me, count, src_of, dst, recv):
        def step(d, carry):
            other = lax.rem(me + d, count)
            copy_to(axis, src_of(other), dst.at[me], recv, me, other, d).start()
            return carry

        lax.fori_loop(1, count, step, 0)

    def wait_all(axis, me, count, src_of, dst, recv, each=None):
        def step(d, carry):
            other = lax.rem(me + d, count)
            copy_to(axis, src_of(other), dst.at[other], recv, other, other, d).wait()
            return carry

        lax.fori_loop(1, count, step, 0)

    col1024 = lax.broadcasted_iota(jnp.int32, (BOX, 1024), 1)
    row32 = lax.broadcasted_iota(jnp.int32, (BOX, 1024), 0)
    inner = inner_ref[...]

    def make_kt(q, carry):
        block = inner * outer_ref[pl.ds(q, 1), :]
        block = jnp.where(col1024 == row32 + q * BOX, 0.0, block)
        kt_s[pl.ds(pl.multiple_of(q * BOX, BOX), BOX), :] = block.astype(BF)
        return carry

    lax.fori_loop(0, BOX, make_kt, 0)

    lane = lax.broadcasted_iota(jnp.int32, (8, 128), 1)
    row8 = lax.broadcasted_iota(jnp.int32, (8, 128), 0)
    hot = jnp.concatenate(
        [jnp.where(lane == row8 + (8 * p - off_ref[0, n] + 32), 1.0, 0.0) for n in range(N_PLN)], axis=0
    ).astype(BF)
    loads[0].wait()
    same = (
        lax.broadcasted_iota(jnp.int32, (128, 512), 0) // 8 == lax.broadcasted_iota(jnp.int32, (128, 512), 1) % N_PLN
    )
    eh = jnp.where(same, dg(hot, depth_ref[0], 1, 0), 0.0).astype(BF)
    el = jnp.where(same, dg(hot, depth_ref[1], 1, 0), 0.0).astype(BF)
    lax.fori_loop(0, BOX, wait_rows, 0)
    x = x_s[...]
    s = dg(eh, x, 1, 0) + dg(el, x, 1, 0)
    psi = main * s + dg(s.astype(BF), kt_s[...], 1, 0)
    psq_s[...] = psi * psi


    def place(n, carry):
        weight = occ_ref[n]
        ox = off_ref[2, n]
        inside = (lane >= ox) & (lane < ox + BOX)
        for bt in range(8):
            v = psq_s[pl.ds(pl.multiple_of(n * 8, 8), 8), bt * 128 : (bt + 1) * 128] * weight
            for j in range(4):
                turned = pltpu.roll(v, lax.rem(ox + 128 - 32 * j, 128), 1)
                at = pl.multiple_of((n * BOX + bt * 4 + j) * 8, 8)
                q_s[pl.ds(at, 8), :] = jnp.where(inside, turned, 0.0)
        return carry

    lax.fori_loop(0, N_PLN, place, 0)

    lane_n = lax.broadcasted_iota(jnp.int32, (1, 512), 1)
    oy = jnp.zeros((1, 512), jnp.int32)
    for n in range(N_PLN):
        oy = jnp.where(lane_n // BOX == n, off_ref[1, n], oy)
    target = oy + lane_n % BOX
    spots = jnp.where(lax.broadcasted_iota(jnp.int32, (G, 512), 0) == target, 1.0, 0.0).astype(BF)
    for i in (3, 4, 5, 6):
        loads[i].wait()
    hh, hl = har_ref[0], har_ref[1]

    def plane(z, carry):
        qz = q_s[pl.ds(z, 512, stride=8), :]
        qh, ql = halves(qz)
        a = dg(spots, qh, 1, 0) + dg(spots, ql, 1, 0)
        d_s[pl.ds(z, 256, stride=8), :] = dot3r(hh, hl, a, 1, 1)
        return carry

    lax.fori_loop(0, 8, plane, 0)
    s1[...] = d_s[...].reshape(N_ORB, 64, 128).astype(BF)

    pl.semaphore_wait(barrier, N_ORB - 1 + N_PLN - 1)
    send_all("orb", o, N_ORB, lambda i: s1.at[i], r1, rs1)

    lane_own = lax.broadcasted_iota(jnp.int32, (BOX, 512), 1) % N_PLN
    oh = jnp.where(lane_own == p, depth_ref[0, 32 : 32 + BOX, :].astype(F32), 0.0).astype(BF)
    ol = jnp.where(lane_own == p, depth_ref[1, 32 : 32 + BOX, :].astype(F32), 0.0).astype(BF)
    s_own = dg(oh, x_s[...], 1, 0) + dg(ol, x_s[...], 1, 0)
    own_s[...] = main * s_own + dg(s_own.astype(BF), kt_s[...], 1, 0)

    for h in range(2):
        d_s[h * 128 : (h + 1) * 128, :] = ker_ref[:, h * 128 : (h + 1) * 128] * (1.0 / float(M) ** 3)
    for kx in range(8):
        for h in range(2):
            kp_s[kx * 16 : (kx + 1) * 16, h * 128 : (h + 1) * 128] = d_s[pl.ds(h * 128 + kx, 16, stride=8), :]

    wait_all("orb", o, N_ORB, lambda i: s1.at[i], r1, rs1)

    def add(d, total):
        return total + r1[lax.rem(o + d, N_ORB)].astype(F32)

    tr = lax.fori_loop(1, N_ORB, add, s1[o].astype(F32))

    y = dot3(tr, hh, hl, 1, 1)
    for i in range(N_PLN):
        total = jnp.zeros((8, 128), F32)
        for kx in range(8):
            v = y[kx * 8 : (kx + 1) * 8, (i // 8) * 128 : (i // 8) * 128 + 128]
            shift = 16 * (kx - i % 8) % 128
            v = pltpu.roll(v, shift, 1) if shift else v
            total = jnp.where(lane // 16 == kx, v, total)
        s2[i] = total
    send_all("pln", p, N_PLN, lambda i: s2.at[i], r2, rs2)
    r2[p] = s2[p]
    wait_all("pln", p, N_PLN, lambda i: s2.at[i], r2, rs2)

    grid_z = r2[...].reshape(G, 128)
    spectrum = dot3(grid_z.T, hh, hl, 1, 1)
    spectrum = spectrum * kp_s[...]
    back_z = dot3r(hart_ref[0], hart_ref[1], spectrum, 1, 1)
    s3[...] = back_z.reshape(N_PLN, 8, 128)
    send_all("pln", p, N_PLN, lambda i: s3.at[i], r3, rs3)
    r3[p] = s3[p]
    wait_all("pln", p, N_PLN, lambda i: s3.at[i], r3, rs3)

    blocks = []
    for kx in range(8):
        sides = []
        for h in range(2):
            total = jnp.zeros((8, 128), F32)
            for i in range(8):
                v = r3[h * 8 + i]
                shift = 16 * (i - kx) % 128
                v = pltpu.roll(v, shift, 1) if shift else v
                total = jnp.where(lane // 16 == i, v, total)
            sides.append(total)
        blocks.append(jnp.concatenate(sides, axis=1))
    w_s[...] = dot3(jnp.concatenate(blocks, axis=0), hh, hl, 1, 0)
    core = lax.rem(o, 2)
    cx, cy = o // 8, lax.rem(o // 2, 4)
    mate = o + 1 - 2 * core

    def peer(step, sign):
        dx, dy = NEAR[step]
        return 8 * lax.rem(cx + sign * dx + 4, 4) + 2 * lax.rem(cy + sign * dy + 4, 4) + core

    def gather(step):
        return copy_to("orb", w_s, r4.at[o], rs4, o, peer(step, 1), step + 1)

    def forward(step):
        src = peer(step, -1)
        return copy_to("orb", r4.at[src], r4.at[src], rs4, src, mate, step + 17)

    first = copy_to("orb", w_s, r4.at[o], rs4, o, mate, 0)
    for step in reversed(range(15)):
        gather(step).start()
    first.start()
    r4[o] = w_s[...]
    for step in range(15):
        src = peer(step, -1)
        copy_to("orb", w_s, r4.at[src], rs4, src, src, step + 1).wait_recv()
        forward(step).start()
    for step in range(15):
        gather(step).wait_send()
    for step in range(15):
        forward(step).wait_send()
        src = peer(step, -1) + 1 - 2 * core
        copy_to("orb", w_s, r4.at[src], rs4, src, mate, step + 17).wait_recv()
    first.wait_send()
    copy_to("orb", w_s, r4.at[mate], rs4, mate, mate, 0).wait_recv()

    d_s[...] = r4[...].reshape(N_ORB * 64, 128)

    def plane_back(z, carry):
        wz = d_s[pl.ds(z, 256, stride=8), :]
        vh, vl = halves(dot3(wz.T, hh, hl, 1, 0))
        q_s[pl.ds(z, 512, stride=8), :] = dg(spots, vh, 0, 0) + dg(spots, vl, 0, 0)
        return carry

    lax.fori_loop(0, 8, plane_back, 0)

    def box(n, carry):
        ox = off_ref[2, n]
        parts = []
        for bt in range(8):
            total = jnp.zeros((8, 128), F32)
            for j in range(4):
                v = q_s[pl.ds(pl.multiple_of((n * BOX + bt * 4 + j) * 8, 8), 8), :]
                v = pltpu.roll(v, lax.rem(128 + 32 * j - ox, 128), 1)
                total = jnp.where(lane // 32 == j, v, total)
            parts.append(total)
        whole = (parts[0] + parts[1] + parts[2] + parts[3]) + (parts[4] + parts[5] + parts[6] + parts[7])
        mean = jnp.broadcast_to(jnp.sum(whole, axis=1, keepdims=True) * (1.0 / 1024), (8, 128)).astype(BF)
        level = mean.astype(F32)
        for bt in range(8):
            s5[n, :, bt * 128 : (bt + 1) * 128] = (parts[bt] - level).astype(BF)
        s5[n, :, 1024:1152] = mean
        return carry

    lax.fori_loop(0, N_PLN, box, 0)
    send_all("pln", p, N_PLN, lambda i: s5.at[i], r5, rs5)
    r5[p] = s5[p]
    wait_all("pln", p, N_PLN, lambda i: s5.at[i], r5, rs5)

    cut = jnp.where(
        lax.broadcasted_iota(jnp.int32, (BOX, G), 1) == lax.broadcasted_iota(jnp.int32, (BOX, G), 0) + off_ref[0, p], 1.0, 0.0
    ).astype(BF)
    picked = dg(cut, r5[...].astype(F32).reshape(G, 1152).astype(BF), 1, 0)
    v_box = picked[:, :1024] + jnp.concatenate([picked[:, 1024:]] * 8, axis=1)
    u = v_box * own_s[...]
    u = main * u + dg(u.astype(BF), kt_s[...], 1, 1)
    f = dot3r(back_ref[0], back_ref[1], u, 1, 0)
    for t in range(16):
        part = f[(t // 8) * 16 : (t // 8) * 16 + 16, (t % 8) * 128 : (t % 8) * 128 + 128]
        fs_s[t * 16 : (t + 1) * 16, :] = part
    for i in range(N_PLN):
        s6[i] = fs_s[pl.ds(i, 16, stride=16), :].astype(BF)
    send_all("pln", p, N_PLN, lambda i: s6.at[i], r6, rs6)
    r6[p] = s6[p]
    wait_all("pln", p, N_PLN, lambda i: s6.at[i], r6, rs6)
    gs_s[...] = r6[...].astype(F32).reshape(256, 128)
    for t in range(16):
        out_ref[:, t * 128 : (t + 1) * 128] = gs_s[pl.ds(t, 16, stride=16), :].astype(BF)


def per_device(orbitals, occupations, box_offsets, kernel_spectrum):
    depth, har, hart, inner, outer, back, main = tables()
    ker = kernel_spectrum.transpose(1, 2, 0).reshape(128, M)
    vm = pl.BlockSpec(memory_space=pltpu.VMEM)
    sm = pl.BlockSpec(memory_space=pltpu.SMEM)
    hbm = pl.BlockSpec(memory_space=pltpu.HBM)
    V = pltpu.VMEM
    dma = pltpu.SemaphoreType.DMA

    def body(*refs):
        kernel(main, *refs)

    return pl.pallas_call(
        body,
        out_shape=jax.ShapeDtypeStruct((16, 2048), BF),
        in_specs=[hbm, sm, sm] + [hbm] * 7,
        out_specs=vm,
        scratch_shapes=[
            V((128, M), F32), V(depth.shape, BF), V(har.shape, BF), V(hart.shape, BF),
            V(inner.shape, F32), V(outer.shape, F32), V(back.shape, BF),
            V((512, 1024), BF),
            V((1024, 1024), BF),
            V((128, 1024), F32),
            V((32, 1024), F32),
            V((4096, 128), F32),
            V((2048, 128), F32),
            V((32, 64, 128), BF),
            V((32, 64, 128), BF),
            V((64, 128), F32),
            V((16, 8, 128), F32),
            V((16, 8, 128), F32),
            V((16, 8, 128), F32),
            V((16, 8, 128), F32),
            V((64, 128), F32),
            V((32, 64, 128), F32),
            V((16, 8, 1152), BF),
            V((16, 8, 1152), BF),
            V((256, 128), F32),
            V((16, 16, 128), BF),
            V((16, 16, 128), BF),
            V((256, 128), F32),
            V((128, 256), F32),
            dma((40,)), dma((32,)), dma((32,)), dma((16,)), dma((16,)), dma((32,)), dma((16,)), dma((16,)),
        ],
        compiler_params=pltpu.CompilerParams(collective_id=0, has_side_effects=True),
        name="hartree",
    )(orbitals, occupations, box_offsets.T, ker, depth, har, hart, inner, outer, back)


def solution(mesh):
    in_specs = (P("orb", None), P("orb"), P("orb", None), P(None, "pln", "orb"))
    out_specs = P("orb", "pln")
    return jax.shard_map(per_device, mesh=mesh, in_specs=in_specs, out_specs=out_specs, check_vma=False)
```

```python
import math

import jax
import jax.numpy as jnp
import numpy as np
from jax import lax
from jax.experimental import pallas as pl
from jax.experimental.pallas import tpu as pltpu
from jax.sharding import PartitionSpec as P

G = 128
BOX = 32
M = 256
N_ORB = 32
N_PLN = 16
UNROLL = 8
BF = jnp.bfloat16
F32 = jnp.float32

MAGIC_TAPS = (
    8.433424733352934e-07,
    -1.290557201342061e-05,
    8.76298447621056e-05,
    -0.00030158038132690465,
    0.001747237136729939,
    -0.009420470302010804,
    0.023738214637249424,
    0.0612625895831208,
    0.9940415697834004,
    -0.06048952891969835,
    -0.021030251609303816,
    0.013372634148547948,
    -0.0034412814449349387,
    0.0004944322768868992,
    -5.185986881173433e-05,
    2.7273449291197967e-06,
)


FAR = sorted(
    [(a, b) for a in range(4) for b in range(4)],
    key=lambda d: -min(d[0], 4 - d[0]) - min(d[1], 4 - d[1]),
)


def split(values):
    high = np.asarray(values, np.float32).astype(BF)
    low = (np.asarray(values, np.float32) - high.astype(np.float32)).astype(BF)
    return np.stack([high, low])


def tables():
    taps = np.asarray(MAGIC_TAPS, np.float32)
    magic = np.zeros((BOX, BOX), np.float32)
    for i in range(BOX):
        for k in range(BOX):
            if -8 <= k - i <= 7:
                magic[i, k] = taps[k - i + 8]
    depth = np.zeros((G, BOX * N_PLN), np.float32)
    depth[32 : 32 + BOX] = np.repeat(magic, N_PLN, axis=1)
    angle = 2.0 * math.pi * (np.outer(np.arange(M), np.arange(G)) % M) / M
    hartley = np.cos(angle) + np.sin(angle)
    inner = np.tile(magic.T, (1, BOX)).astype(np.float32)
    outer = np.repeat(magic.T, BOX, axis=1).astype(np.float32)
    back = np.concatenate([magic[:, 0::2].T, magic[:, 1::2].T])
    return split(depth), split(hartley), split(hartley.T), inner, outer, split(back), float(magic[0, 0]) ** 2


def dg(a, b, ca, cb):
    return lax.dot_general(a, b, (((ca,), (cb,)), ((), ())), preferred_element_type=F32)


def halves(a):
    high = a.astype(BF)
    return high, (a - high.astype(F32)).astype(BF)


def dot3(a, bh, bl, ca, cb):
    ah, al = halves(a)
    return dg(ah, bh, ca, cb) + (dg(al, bh, ca, cb) + dg(ah, bl, ca, cb))


def dot3r(ah, al, b, ca, cb):
    bh, bl = halves(b)
    return dg(ah, bh, ca, cb) + (dg(al, bh, ca, cb) + dg(ah, bl, ca, cb))


def kernel(
    main,
    orb_hbm, occ_ref, off_ref, ker_hbm, depth_hbm, har_hbm, hart_hbm, inner_hbm, outer_hbm, back_hbm,
    out_ref,
    ker_ref, depth_ref, har_ref, hart_ref, inner_ref, outer_ref, back_ref,
    x_s, kt_s, psq_s, own_s, q_s, d_s, s1, r1, m1, mr1, s2, r2, s3, r3, w_s, r4, s5, r5, fs_s, s6, r6, gs_s, kp_s,
    load_sem, send_sem, rsm, rs1, rs2, rs3, rs4, rs5, rs6,
):
    o = lax.axis_index("orb")
    p = lax.axis_index("pln")
    barrier = pltpu.get_barrier_semaphore()

    def greet(axis, me, count):
        def step(d, carry):
            pl.semaphore_signal(
                barrier, inc=1, device_id={axis: lax.rem(me + d, count)}, device_id_type=pl.DeviceIdType.MESH
            )
            return carry

        lax.fori_loop(1, count, step, 0)

    greet("orb", o, N_ORB)
    greet("pln", p, N_PLN)

    pairs = (
        (depth_hbm, depth_ref), (inner_hbm, inner_ref), (outer_hbm, outer_ref), (har_hbm, har_ref),
        (ker_hbm, ker_ref), (hart_hbm, hart_ref), (back_hbm, back_ref),
    )
    loads = [pltpu.make_async_copy(a, b, load_sem.at[i]) for i, (a, b) in enumerate(pairs)]
    rows_of = lambda k: pltpu.make_async_copy(
        orb_hbm.at[:, pl.ds(pl.multiple_of(k * 1024, 1024), 1024)],
        x_s.at[pl.ds(pl.multiple_of(k * 16, 16), 16), :],
        load_sem.at[8 + k],
    )

    def start_rows(k, carry):
        rows_of(k).start()
        return carry

    def wait_rows(k, carry):
        rows_of(k).wait()
        return carry

    for i in (1, 2, 0):
        loads[i].start()
    lax.fori_loop(0, BOX, start_rows, 0)
    for i in (3, 4, 5, 6):
        loads[i].start()
    loads[1].wait()
    loads[2].wait()

    def copy_to(axis, src, dst, recv, slot, other, sem_slot):
        return pltpu.make_async_remote_copy(
            src_ref=src, dst_ref=dst, send_sem=send_sem.at[sem_slot], recv_sem=recv.at[slot],
            device_id={axis: other}, device_id_type=pl.DeviceIdType.MESH,
        )

    def far(i):
        return lax.rem(p + 8 + (1 - 2 * lax.rem(i, 2)) * ((i + 1) // 2), N_PLN)

    def send_all(axis, me, count, src_of, dst, recv):
        def step(i, carry):
            other = far(i)
            copy_to(axis, src_of(other), dst.at[me], recv, me, other, i).start()
            return carry

        lax.fori_loop(0, count - 1, step, 0)

    def wait_all(axis, me, count, src_of, dst, recv):
        def step(i, carry):
            other = far(count - 2 - i)
            copy_to(axis, src_of(other), dst.at[other], recv, other, other, i).wait()
            return carry

        lax.fori_loop(0, count - 1, step, 0)

    col1024 = lax.broadcasted_iota(jnp.int32, (BOX, 1024), 1)
    row32 = lax.broadcasted_iota(jnp.int32, (BOX, 1024), 0)
    inner = inner_ref[...]

    def make_kt(q, carry):
        block = inner * outer_ref[pl.ds(q, 1), :]
        block = jnp.where(col1024 == row32 + q * BOX, 0.0, block)
        kt_s[pl.ds(pl.multiple_of(q * BOX, BOX), BOX), :] = block.astype(BF)
        return carry

    lax.fori_loop(0, BOX, make_kt, 0)

    lane = lax.broadcasted_iota(jnp.int32, (8, 128), 1)
    row8 = lax.broadcasted_iota(jnp.int32, (8, 128), 0)
    hot = jnp.concatenate(
        [jnp.where(lane == row8 + (8 * p - off_ref[0, n] + 32), 1.0, 0.0) for n in range(N_PLN)], axis=0
    ).astype(BF)
    loads[0].wait()
    same = (
        lax.broadcasted_iota(jnp.int32, (128, 512), 0) // 8 == lax.broadcasted_iota(jnp.int32, (128, 512), 1) % N_PLN
    )
    eh = jnp.where(same, dg(hot, depth_ref[0], 1, 0), 0.0).astype(BF)
    el = jnp.where(same, dg(hot, depth_ref[1], 1, 0), 0.0).astype(BF)
    lax.fori_loop(0, BOX, wait_rows, 0)
    x = x_s[...]
    s = dg(eh, x, 1, 0) + dg(el, x, 1, 0)
    psi = main * s + dg(s.astype(BF), kt_s[...], 1, 0)
    psq_s[...] = psi * psi


    def place(n, carry):
        weight = occ_ref[n]
        ox = off_ref[2, n]
        inside = (lane >= ox) & (lane < ox + BOX)
        for bt in range(8):
            v = psq_s[pl.ds(pl.multiple_of(n * 8, 8), 8), bt * 128 : (bt + 1) * 128] * weight
            for j in range(4):
                turned = pltpu.roll(v, lax.rem(ox + 128 - 32 * j, 128), 1)
                at = pl.multiple_of((n * BOX + bt * 4 + j) * 8, 8)
                q_s[pl.ds(at, 8), :] = jnp.where(inside, turned, 0.0)
        return carry

    lax.fori_loop(0, N_PLN, place, 0)

    lane_n = lax.broadcasted_iota(jnp.int32, (1, 512), 1)
    oy = jnp.zeros((1, 512), jnp.int32)
    for n in range(N_PLN):
        oy = jnp.where(lane_n // BOX == n, off_ref[1, n], oy)
    target = oy + lane_n % BOX
    spots = jnp.where(lax.broadcasted_iota(jnp.int32, (G, 512), 0) == target, 1.0, 0.0).astype(BF)
    for i in (3, 4, 5, 6):
        loads[i].wait()
    hh, hl = har_ref[0], har_ref[1]

    def plane(z, carry):
        qz = q_s[pl.ds(z, 512, stride=8), :]
        qh, ql = halves(qz)
        a = dg(spots, qh, 1, 0) + dg(spots, ql, 1, 0)
        d_s[pl.ds(z, 256, stride=8), :] = dot3r(hh, hl, a, 1, 1)
        return carry

    lax.fori_loop(0, 8, plane, 0, unroll=UNROLL)

    core = lax.rem(o, 2)
    cx, cy = o // 8, lax.rem(o // 2, 4)
    mate = o + 1 - 2 * core
    here = o // 2

    def chip(step, sign):
        dx, dy = FAR[step]
        return 4 * lax.rem(cx + sign * dx + 4, 4) + lax.rem(cy + sign * dy + 4, 4)

    def block(owner):
        return d_s[pl.ds(pl.multiple_of(owner * 64, 64), 64), :]

    def to_mate(part):
        rows = pl.ds(part * 8, 8)
        return copy_to("orb", m1.at[rows], mr1.at[rows], rsm, part, mate, 30 + part)

    def to_chip(step):
        return copy_to("orb", s1.at[step], r1.at[here], rs1, here, 2 * chip(step, 1) + core, step)

    def from_chip(step):
        src = chip(step, -1)
        return copy_to("orb", s1.at[step], r1.at[src], rs1, src, 2 * src + core, step)

    for step in range(16):
        m1[step] = block(2 * chip(step, 1) + 1 - core).astype(BF)
        if step == 7:
            pl.semaphore_wait(barrier, N_ORB - 1 + N_PLN - 1)
            to_mate(0).start()
    to_mate(1).start()
    for step in range(15):
        if step % 8 == 0:
            to_mate(step // 8).wait()
        s1[step] = (block(2 * chip(step, 1) + core) + mr1[step].astype(F32)).astype(BF)
        to_chip(step).start()
    tr = block(o) + mr1[15].astype(F32)

    lane_own = lax.broadcasted_iota(jnp.int32, (BOX, 512), 1) % N_PLN
    oh = jnp.where(lane_own == p, depth_ref[0, 32 : 32 + BOX, :].astype(F32), 0.0).astype(BF)
    ol = jnp.where(lane_own == p, depth_ref[1, 32 : 32 + BOX, :].astype(F32), 0.0).astype(BF)
    s_own = dg(oh, x_s[...], 1, 0) + dg(ol, x_s[...], 1, 0)
    own_s[...] = main * s_own + dg(s_own.astype(BF), kt_s[...], 1, 0)

    for h in range(2):
        d_s[h * 128 : (h + 1) * 128, :] = ker_ref[:, h * 128 : (h + 1) * 128] * (1.0 / float(M) ** 3)
    for kx in range(8):
        for h in range(2):
            kp_s[kx * 16 : (kx + 1) * 16, h * 128 : (h + 1) * 128] = d_s[pl.ds(h * 128 + kx, 16, stride=8), :]

    for step in reversed(range(15)):
        from_chip(step).wait()
        tr = tr + r1[chip(step, -1)].astype(F32)

    y = dot3(tr, hh, hl, 1, 1)
    for i in range(N_PLN):
        total = jnp.zeros((8, 128), F32)
        for kx in range(8):
            v = y[kx * 8 : (kx + 1) * 8, (i // 8) * 128 : (i // 8) * 128 + 128]
            shift = 16 * (kx - i % 8) % 128
            v = pltpu.roll(v, shift, 1) if shift else v
            total = jnp.where(lane // 16 == kx, v, total)
        s2[i] = total
    send_all("pln", p, N_PLN, lambda i: s2.at[i], r2, rs2)
    r2[p] = s2[p]
    wait_all("pln", p, N_PLN, lambda i: s2.at[i], r2, rs2)

    grid_z = r2[...].reshape(G, 128)
    spectrum = dot3(grid_z.T, hh, hl, 1, 1)
    spectrum = spectrum * kp_s[...]
    back_z = dot3r(hart_ref[0], hart_ref[1], spectrum, 1, 1)
    s3[...] = back_z.reshape(N_PLN, 8, 128)
    send_all("pln", p, N_PLN, lambda i: s3.at[i], r3, rs3)
    r3[p] = s3[p]
    wait_all("pln", p, N_PLN, lambda i: s3.at[i], r3, rs3)

    blocks = []
    for kx in range(8):
        sides = []
        for h in range(2):
            total = jnp.zeros((8, 128), F32)
            for i in range(8):
                v = r3[h * 8 + i]
                shift = 16 * (i - kx) % 128
                v = pltpu.roll(v, shift, 1) if shift else v
                total = jnp.where(lane // 16 == i, v, total)
            sides.append(total)
        blocks.append(jnp.concatenate(sides, axis=1))
    w_s[...] = dot3(jnp.concatenate(blocks, axis=0), hh, hl, 1, 0)
    def gather(step):
        return copy_to("orb", w_s, r4.at[o], rs4, o, 2 * chip(step, 1) + core, step)

    def arrive(step):
        src = 2 * chip(step, -1) + core
        return copy_to("orb", w_s, r4.at[src], rs4, src, src, step)

    def forward(step):
        src = 2 * chip(step, -1) + core
        return copy_to("orb", r4.at[src], r4.at[src], rs4, src, mate, step + 16)

    def passed(step):
        src = 2 * chip(step, -1) + 1 - core
        return copy_to("orb", w_s, r4.at[src], rs4, src, mate, step + 16)

    first = copy_to("orb", w_s, r4.at[o], rs4, o, mate, 15)
    for step in range(15):
        gather(step).start()
    first.start()
    r4[o] = w_s[...]
    for step in reversed(range(15)):
        arrive(step).wait_recv()
        forward(step).start()
    for step in range(15):
        gather(step).wait_send()
    first.wait_send()
    for step in reversed(range(16)):
        passed(step).wait_recv()
        if step < 15:
            forward(step).wait_send()

    d_s[...] = r4[...].reshape(N_ORB * 64, 128)

    def plane_back(z, carry):
        wz = d_s[pl.ds(z, 256, stride=8), :]
        vh, vl = halves(dot3(wz.T, hh, hl, 1, 0))
        q_s[pl.ds(z, 512, stride=8), :] = dg(spots, vh, 0, 0) + dg(spots, vl, 0, 0)
        return carry

    lax.fori_loop(0, 8, plane_back, 0, unroll=UNROLL)

    def send_box(i):
        n = far(i)
        return copy_to("pln", s5.at[n], r5.at[p], rs5, p, n, i)

    def box(i, carry):
        n = far(i)
        ox = off_ref[2, n]
        parts = []
        for bt in range(8):
            total = jnp.zeros((8, 128), F32)
            for j in range(4):
                v = q_s[pl.ds(pl.multiple_of((n * BOX + bt * 4 + j) * 8, 8), 8), :]
                v = pltpu.roll(v, lax.rem(128 + 32 * j - ox, 128), 1)
                total = jnp.where(lane // 32 == j, v, total)
            parts.append(total)
        whole = (parts[0] + parts[1] + parts[2] + parts[3]) + (parts[4] + parts[5] + parts[6] + parts[7])
        mean = jnp.broadcast_to(jnp.sum(whole, axis=1, keepdims=True) * (1.0 / 1024), (8, 128)).astype(BF)
        level = mean.astype(F32)
        for bt in range(8):
            s5[n, :, bt * 128 : (bt + 1) * 128] = (parts[bt] - level).astype(BF)
        s5[n, :, 1024:1152] = mean
        return carry

    def box_out(i, carry):
        box(i, carry)
        send_box(i).start()
        return carry

    lax.fori_loop(0, N_PLN - 1, box_out, 0)
    box(N_PLN - 1, 0)
    r5[p] = s5[p]
    wait_all("pln", p, N_PLN, lambda i: s5.at[i], r5, rs5)

    cut = jnp.where(
        lax.broadcasted_iota(jnp.int32, (BOX, G), 1) == lax.broadcasted_iota(jnp.int32, (BOX, G), 0) + off_ref[0, p], 1.0, 0.0
    ).astype(BF)
    picked = dg(cut, r5[...].astype(F32).reshape(G, 1152).astype(BF), 1, 0)
    v_box = picked[:, :1024] + jnp.concatenate([picked[:, 1024:]] * 8, axis=1)
    u = v_box * own_s[...]
    u = main * u + dg(u.astype(BF), kt_s[...], 1, 1)
    f = dot3r(back_ref[0], back_ref[1], u, 1, 0)
    for t in range(16):
        part = f[(t // 8) * 16 : (t // 8) * 16 + 16, (t % 8) * 128 : (t % 8) * 128 + 128]
        fs_s[t * 16 : (t + 1) * 16, :] = part
    for i in range(N_PLN):
        s6[i] = fs_s[pl.ds(i, 16, stride=16), :].astype(BF)
    send_all("pln", p, N_PLN, lambda i: s6.at[i], r6, rs6)
    r6[p] = s6[p]
    wait_all("pln", p, N_PLN, lambda i: s6.at[i], r6, rs6)
    gs_s[...] = r6[...].astype(F32).reshape(256, 128)
    for t in range(16):
        out_ref[:, t * 128 : (t + 1) * 128] = gs_s[pl.ds(t, 16, stride=16), :].astype(BF)


def per_device(orbitals, occupations, box_offsets, kernel_spectrum):
    depth, har, hart, inner, outer, back, main = tables()
    ker = kernel_spectrum.transpose(1, 2, 0).reshape(128, M)
    vm = pl.BlockSpec(memory_space=pltpu.VMEM)
    sm = pl.BlockSpec(memory_space=pltpu.SMEM)
    hbm = pl.BlockSpec(memory_space=pltpu.HBM)
    V = pltpu.VMEM
    dma = pltpu.SemaphoreType.DMA

    def body(*refs):
        kernel(main, *refs)

    return pl.pallas_call(
        body,
        out_shape=jax.ShapeDtypeStruct((16, 2048), BF),
        in_specs=[hbm, sm, sm] + [hbm] * 7,
        out_specs=vm,
        scratch_shapes=[
            V((128, M), F32), V(depth.shape, BF), V(har.shape, BF), V(hart.shape, BF),
            V(inner.shape, F32), V(outer.shape, F32), V(back.shape, BF),
            V((512, 1024), BF),
            V((1024, 1024), BF),
            V((128, 1024), F32),
            V((32, 1024), F32),
            V((4096, 128), F32),
            V((2048, 128), F32),
            V((16, 64, 128), BF),
            V((16, 64, 128), BF),
            V((16, 64, 128), BF),
            V((16, 64, 128), BF),
            V((16, 8, 128), F32),
            V((16, 8, 128), F32),
            V((16, 8, 128), F32),
            V((16, 8, 128), F32),
            V((64, 128), F32),
            V((32, 64, 128), F32),
            V((16, 8, 1152), BF),
            V((16, 8, 1152), BF),
            V((256, 128), F32),
            V((16, 16, 128), BF),
            V((16, 16, 128), BF),
            V((256, 128), F32),
            V((128, 256), F32),
            dma((40,)), dma((32,)), dma((2,)), dma((16,)), dma((16,)), dma((16,)), dma((32,)), dma((16,)), dma((16,)),
        ],
        compiler_params=pltpu.CompilerParams(collective_id=0, has_side_effects=True),
        name="hartree",
    )(orbitals, occupations, box_offsets.T, ker, depth, har, hart, inner, outer, back)


def solution(mesh):
    in_specs = (P("orb", None), P("orb"), P("orb", None), P(None, "pln", "orb"))
    out_specs = P("orb", "pln")
    return jax.shard_map(per_device, mesh=mesh, in_specs=in_specs, out_specs=out_specs, check_vma=False)
```

```python
import math

import jax
import jax.numpy as jnp
import numpy as np
from jax import lax
from jax.experimental import pallas as pl
from jax.experimental.pallas import tpu as pltpu
from jax.sharding import PartitionSpec as P

G = 128
BOX = 32
M = 256
N_ORB = 32
N_PLN = 16
BF = jnp.bfloat16
F32 = jnp.float32

MAGIC_TAPS = (
    8.433424733352934e-07,
    -1.290557201342061e-05,
    8.76298447621056e-05,
    -0.00030158038132690465,
    0.001747237136729939,
    -0.009420470302010804,
    0.023738214637249424,
    0.0612625895831208,
    0.9940415697834004,
    -0.06048952891969835,
    -0.021030251609303816,
    0.013372634148547948,
    -0.0034412814449349387,
    0.0004944322768868992,
    -5.185986881173433e-05,
    2.7273449291197967e-06,
)


FAR = sorted(
    [(a, b) for a in range(4) for b in range(4)],
    key=lambda d: -min(d[0], 4 - d[0]) - min(d[1], 4 - d[1]),
)


def split(values):
    high = np.asarray(values, np.float32).astype(BF)
    low = (np.asarray(values, np.float32) - high.astype(np.float32)).astype(BF)
    return np.stack([high, low])


def tables():
    taps = np.asarray(MAGIC_TAPS, np.float32)
    magic = np.zeros((BOX, BOX), np.float32)
    for i in range(BOX):
        for k in range(BOX):
            if -8 <= k - i <= 7:
                magic[i, k] = taps[k - i + 8]
    depth = np.repeat(magic, N_PLN, axis=1)
    angle = 2.0 * math.pi * (np.outer(np.arange(M), np.arange(G)) % M) / M
    hartley = np.cos(angle) + np.sin(angle)
    cyclic = np.arange(G).reshape(8, N_PLN).T.reshape(-1)
    inner = np.tile(magic.T, (1, BOX)).astype(np.float32)
    outer = np.repeat(magic.T, BOX, axis=1).astype(np.float32)
    back = np.concatenate([magic[:, 0::2].T, magic[:, 1::2].T])
    return split(depth), split(hartley), split(hartley.T), split(hartley[:, cyclic]), split(hartley.T[cyclic]), inner, outer, split(back), float(magic[0, 0]) ** 2


def dg(a, b, ca, cb):
    return lax.dot_general(a, b, (((ca,), (cb,)), ((), ())), preferred_element_type=F32)


def halves(a):
    high = a.astype(BF)
    return high, (a - high.astype(F32)).astype(BF)


def dot3(a, bh, bl, ca, cb):
    ah, al = halves(a)
    return dg(ah, bh, ca, cb) + (dg(al, bh, ca, cb) + dg(ah, bl, ca, cb))


def dot3r(ah, al, b, ca, cb):
    bh, bl = halves(b)
    return dg(ah, bh, ca, cb) + (dg(al, bh, ca, cb) + dg(ah, bl, ca, cb))


def kernel(
    main,
    orb_hbm, occ_ref, off_ref, ker_hbm, depth_hbm, har_hbm, hart_hbm, harz_hbm, hartz_hbm, inner_hbm, outer_hbm, back_hbm,
    out_ref,
    ker_ref, depth_ref, har_ref, hart_ref, harz_ref, hartz_ref, inner_ref, outer_ref, back_ref,
    x_s, kt_s, psq_s, own_s, q_s, oh_s, d_s, s1, r1, m1, mr1, s2, r2, s3, r3, w_s, r4, s5, r5, fs_s, s6, r6, gs_s, kp_s,
    load_sem, send_sem, rsm, rs1, rs2, rs3, rs4, rs5, rs6,
):
    o = lax.axis_index("orb")
    p = lax.axis_index("pln")
    barrier = pltpu.get_barrier_semaphore()

    def greet(axis, me, count):
        def step(d, carry):
            pl.semaphore_signal(
                barrier, inc=1, device_id={axis: lax.rem(me + d, count)}, device_id_type=pl.DeviceIdType.MESH
            )
            return carry

        lax.fori_loop(1, count, step, 0)

    greet("orb", o, N_ORB)
    greet("pln", p, N_PLN)

    pairs = (
        (depth_hbm, depth_ref), (inner_hbm, inner_ref), (outer_hbm, outer_ref), (har_hbm, har_ref),
        (ker_hbm, ker_ref), (hart_hbm, hart_ref), (back_hbm, back_ref), (harz_hbm, harz_ref), (hartz_hbm, hartz_ref),
    )
    loads = [pltpu.make_async_copy(a, b, load_sem.at[i]) for i, (a, b) in enumerate(pairs)]
    rows_of = lambda k: pltpu.make_async_copy(
        orb_hbm.at[:, pl.ds(pl.multiple_of(k * 1024, 1024), 1024)],
        x_s.at[pl.ds(pl.multiple_of(k * 16, 16), 16), :],
        load_sem.at[12 + k],
    )

    def start_rows(k, carry):
        rows_of(k).start()
        return carry

    def wait_rows(k, carry):
        rows_of(k).wait()
        return carry

    for i in (1, 2, 0):
        loads[i].start()
    lax.fori_loop(0, BOX, start_rows, 0)
    for i in range(3, 9):
        loads[i].start()
    loads[1].wait()
    loads[2].wait()

    def copy_to(axis, src, dst, recv, slot, other, sem_slot):
        return pltpu.make_async_remote_copy(
            src_ref=src, dst_ref=dst, send_sem=send_sem.at[sem_slot], recv_sem=recv.at[slot],
            device_id={axis: other}, device_id_type=pl.DeviceIdType.MESH,
        )

    def far(i):
        return lax.rem(p + 8 + (1 - 2 * lax.rem(i, 2)) * ((i + 1) // 2), N_PLN)

    def send_all(axis, me, count, src_of, dst, recv):
        def step(i, carry):
            other = far(i)
            copy_to(axis, src_of(other), dst.at[me], recv, me, other, i).start()
            return carry

        lax.fori_loop(0, count - 1, step, 0)

    def wait_all(axis, me, count, src_of, dst, recv):
        def step(i, carry):
            other = far(count - 2 - i)
            copy_to(axis, src_of(other), dst.at[other], recv, other, other, i).wait()
            return carry

        lax.fori_loop(0, count - 1, step, 0)

    col1024 = lax.broadcasted_iota(jnp.int32, (BOX, 1024), 1)
    row32 = lax.broadcasted_iota(jnp.int32, (BOX, 1024), 0)
    inner = inner_ref[...]

    def make_kt(q, carry):
        block = inner * outer_ref[pl.ds(q, 1), :]
        block = jnp.where(col1024 == row32 + q * BOX, 0.0, block)
        kt_s[pl.ds(pl.multiple_of(q * BOX, BOX), BOX), :] = block.astype(BF)
        return carry

    lax.fori_loop(0, BOX, make_kt, 0)

    lane = lax.broadcasted_iota(jnp.int32, (8, 128), 1)
    row = lax.broadcasted_iota(jnp.int32, (BOX, BOX), 0)
    col = lax.broadcasted_iota(jnp.int32, (BOX, BOX), 1)
    first_plane = jnp.zeros((BOX, BOX), jnp.int32)
    for n in range(N_PLN):
        first_plane = jnp.where(row // 2 == n, (p - off_ref[0, n] + 128) & 15, first_plane)
    hot = jnp.where(col == first_plane + 16 * (row % 2), 1.0, 0.0).astype(BF)
    loads[0].wait()
    lane512 = lax.broadcasted_iota(jnp.int32, (BOX, 512), 1) % N_PLN
    same = lax.broadcasted_iota(jnp.int32, (BOX, 512), 0) // 2 == lane512
    eh = jnp.where(same, dg(hot, depth_ref[0], 1, 0), 0.0).astype(BF)
    el = jnp.where(same, dg(hot, depth_ref[1], 1, 0), 0.0).astype(BF)
    lax.fori_loop(0, BOX, wait_rows, 0)
    x = x_s[...]
    s = dg(eh, x, 1, 0) + dg(el, x, 1, 0)
    psi = main * s + dg(s.astype(BF), kt_s[...], 1, 0)
    psi = psi * psi
    for t in range(8):
        psq_s[t * BOX : (t + 1) * BOX, :] = psi[:, t * 128 : (t + 1) * 128]

    pattern = lax.broadcasted_iota(jnp.int32, (BOX, 1024), 0)
    pattern = 4 * (pattern % 8) + pattern // 8

    def place(n, carry):
        weight = occ_ref[n]
        ox = off_ref[2, n]
        oz = off_ref[0, n]
        inside = (lane >= ox) & (lane < ox + BOX)
        plane = (oz + ((p - oz + 128) & 15) - p) >> 4
        for h in range(2):
            v = psq_s[pl.ds(n * 2 + h, 8, stride=BOX), :] * weight
            for j in range(4):
                turned = pltpu.roll(v, lax.rem(ox + 128 - 32 * j, 128), 1)
                at = pl.multiple_of(((n * 2 + h) * 4 + j) * 8, 8)
                q_s[pl.ds(at, 8), :] = jnp.where(inside, turned, 0.0)
            base = (plane + h) * G + off_ref[1, n]
            at = pl.multiple_of((n * 2 + h) * BOX, BOX)
            oh_s[pl.ds(at, BOX), :] = jnp.where(col1024 == pattern + base, 1.0, 0.0).astype(BF)
        return carry

    lax.fori_loop(0, N_PLN, place, 0)

    for i in range(3, 9):
        loads[i].wait()
    hh, hl = har_ref[0], har_ref[1]
    qh, ql = halves(q_s[...])
    both = dg(jnp.concatenate([qh, ql], axis=1), oh_s[...], 0, 0)
    planes = both[:G] + both[G:]
    d = dot3r(hh, hl, planes, 1, 0)
    for z in range(8):
        d_s[pl.ds(z, 256, stride=8), :] = d[:, z * 128 : (z + 1) * 128]

    core = lax.rem(o, 2)
    cx, cy = o // 8, lax.rem(o // 2, 4)
    mate = o + 1 - 2 * core
    here = o // 2

    def chip(step, sign):
        dx, dy = FAR[step]
        return 4 * lax.rem(cx + sign * dx + 4, 4) + lax.rem(cy + sign * dy + 4, 4)

    def block(owner):
        return d_s[pl.ds(pl.multiple_of(owner * 64, 64), 64), :]

    def to_mate(part):
        rows = pl.ds(part * 8, 8)
        return copy_to("orb", m1.at[rows], mr1.at[rows], rsm, part, mate, 30 + part)

    def to_chip(step):
        return copy_to("orb", s1.at[step], r1.at[here], rs1, here, 2 * chip(step, 1) + core, step)

    def from_chip(step):
        src = chip(step, -1)
        return copy_to("orb", s1.at[step], r1.at[src], rs1, src, 2 * src + core, step)

    for step in range(16):
        m1[step] = block(2 * chip(step, 1) + 1 - core).astype(BF)
        if step == 7:
            pl.semaphore_wait(barrier, N_ORB - 1 + N_PLN - 1)
            to_mate(0).start()
    to_mate(1).start()
    for step in range(15):
        if step % 8 == 0:
            to_mate(step // 8).wait()
        s1[step] = (block(2 * chip(step, 1) + core) + mr1[step].astype(F32)).astype(BF)
        to_chip(step).start()
    tr = block(o) + mr1[15].astype(F32)

    oz_own = off_ref[0, p]
    own_hot = jnp.where(col == ((row // 2 - oz_own + 128) & 15) + 16 * (row % 2), 1.0, 0.0).astype(BF)
    oh = jnp.where(lane512 == p, dg(own_hot, depth_ref[0], 1, 0), 0.0).astype(BF)
    ol = jnp.where(lane512 == p, dg(own_hot, depth_ref[1], 1, 0), 0.0).astype(BF)
    back_h = dg(back_ref[0], own_hot, 1, 1).astype(BF)
    back_l = dg(back_ref[1], own_hot, 1, 1).astype(BF)
    s_own = dg(oh, x_s[...], 1, 0) + dg(ol, x_s[...], 1, 0)
    own_s[...] = main * s_own + dg(s_own.astype(BF), kt_s[...], 1, 0)

    for h in range(2):
        d_s[h * 128 : (h + 1) * 128, :] = ker_ref[:, h * 128 : (h + 1) * 128] * (1.0 / float(M) ** 3)
    for kx in range(8):
        for h in range(2):
            kp_s[kx * 16 : (kx + 1) * 16, h * 128 : (h + 1) * 128] = d_s[pl.ds(h * 128 + kx, 16, stride=8), :]

    for step in reversed(range(15)):
        from_chip(step).wait()
        tr = tr + r1[chip(step, -1)].astype(F32)

    y = dot3(tr, hh, hl, 1, 1)
    for i in range(N_PLN):
        total = jnp.zeros((8, 128), F32)
        for kx in range(8):
            v = y[kx * 8 : (kx + 1) * 8, (i // 8) * 128 : (i // 8) * 128 + 128]
            shift = 16 * (kx - i % 8) % 128
            v = pltpu.roll(v, shift, 1) if shift else v
            total = jnp.where(lane // 16 == kx, v, total)
        s2[i] = total
    send_all("pln", p, N_PLN, lambda i: s2.at[i], r2, rs2)
    r2[p] = s2[p]
    wait_all("pln", p, N_PLN, lambda i: s2.at[i], r2, rs2)

    grid_z = r2[...].reshape(G, 128)
    spectrum = dot3(grid_z.T, harz_ref[0], harz_ref[1], 1, 1)
    spectrum = spectrum * kp_s[...]
    back_z = dot3r(hartz_ref[0], hartz_ref[1], spectrum, 1, 1)
    s3[...] = back_z.reshape(N_PLN, 8, 128)
    send_all("pln", p, N_PLN, lambda i: s3.at[i], r3, rs3)
    r3[p] = s3[p]
    wait_all("pln", p, N_PLN, lambda i: s3.at[i], r3, rs3)

    blocks = []
    for kx in range(8):
        sides = []
        for h in range(2):
            total = jnp.zeros((8, 128), F32)
            for i in range(8):
                v = r3[h * 8 + i]
                shift = 16 * (i - kx) % 128
                v = pltpu.roll(v, shift, 1) if shift else v
                total = jnp.where(lane // 16 == i, v, total)
            sides.append(total)
        blocks.append(jnp.concatenate(sides, axis=1))
    w_s[...] = dot3(jnp.concatenate(blocks, axis=0), hh, hl, 1, 0)
    def gather(step):
        return copy_to("orb", w_s, r4.at[o], rs4, o, 2 * chip(step, 1) + core, step)

    def arrive(step):
        src = 2 * chip(step, -1) + core
        return copy_to("orb", w_s, r4.at[src], rs4, src, src, step)

    def forward(step):
        src = 2 * chip(step, -1) + core
        return copy_to("orb", r4.at[src], r4.at[src], rs4, src, mate, step + 16)

    def passed(step):
        src = 2 * chip(step, -1) + 1 - core
        return copy_to("orb", w_s, r4.at[src], rs4, src, mate, step + 16)

    first = copy_to("orb", w_s, r4.at[o], rs4, o, mate, 15)
    for step in range(15):
        gather(step).start()
    first.start()
    r4[o] = w_s[...]
    for step in reversed(range(15)):
        arrive(step).wait_recv()
        forward(step).start()
    for step in range(15):
        gather(step).wait_send()
    first.wait_send()
    for step in reversed(range(16)):
        passed(step).wait_recv()
        if step < 15:
            forward(step).wait_send()

    d_s[...] = r4[...].reshape(N_ORB * 64, 128)

    w = jnp.concatenate([d_s[pl.ds(z, 256, stride=8), :] for z in range(8)], axis=1)
    v = dot3r(hart_ref[0], hart_ref[1], w, 1, 0)
    vh, vl = halves(v)
    both = dg(oh_s[...], jnp.concatenate([vh, vl], axis=0), 1, 1)
    q_s[...] = both[:, :G] + both[:, G:]

    def rows16(i):
        return pl.ds(pl.multiple_of(i * 16, 16), 16)

    def send_box(i):
        n = far(i)
        return copy_to("pln", s5.at[rows16(n)], r5.at[rows16(p)], rs5, p, n, i)

    def wait_box(i, carry):
        n = far(N_PLN - 2 - i)
        copy_to("pln", s5.at[rows16(n)], r5.at[rows16(n)], rs5, n, n, i).wait()
        return carry

    def box(n, put):
        ox = off_ref[2, n]
        for h in range(2):
            total = jnp.zeros((8, 128), F32)
            for j in range(4):
                u = q_s[pl.ds(pl.multiple_of(((n * 2 + h) * 4 + j) * 8, 8), 8), :]
                u = pltpu.roll(u, lax.rem(128 + 32 * j - ox, 128), 1)
                total = jnp.where(lane // 32 == j, u, total)
            put[pl.ds(pl.multiple_of(n * 16 + h * 8, 8), 8), :] = total

    def box_out(i, carry):
        box(far(i), s5)
        send_box(i).start()
        return carry

    lax.fori_loop(0, N_PLN - 1, box_out, 0)
    box(p, r5)
    lax.fori_loop(0, N_PLN - 1, wait_box, 0)

    own = own_s[...]
    u = jnp.concatenate(
        [r5[pl.ds(t, BOX, stride=8), :] * own[:, t * 128 : (t + 1) * 128] for t in range(8)], axis=1
    )
    u = main * u + dg(u.astype(BF), kt_s[...], 1, 1)
    f = dot3r(back_h, back_l, u, 1, 0)
    for t in range(16):
        part = f[(t // 8) * 16 : (t // 8) * 16 + 16, (t % 8) * 128 : (t % 8) * 128 + 128]
        fs_s[t * 16 : (t + 1) * 16, :] = part
    for i in range(N_PLN):
        s6[i] = fs_s[pl.ds(i, 16, stride=16), :].astype(BF)
    send_all("pln", p, N_PLN, lambda i: s6.at[i], r6, rs6)
    r6[p] = s6[p]
    wait_all("pln", p, N_PLN, lambda i: s6.at[i], r6, rs6)
    gs_s[...] = r6[...].astype(F32).reshape(256, 128)
    for t in range(16):
        out_ref[:, t * 128 : (t + 1) * 128] = gs_s[pl.ds(t, 16, stride=16), :].astype(BF)


def per_device(orbitals, occupations, box_offsets, kernel_spectrum):
    depth, har, hart, harz, hartz, inner, outer, back, main = tables()
    ker = kernel_spectrum.transpose(1, 2, 0).reshape(128, M)
    vm = pl.BlockSpec(memory_space=pltpu.VMEM)
    sm = pl.BlockSpec(memory_space=pltpu.SMEM)
    hbm = pl.BlockSpec(memory_space=pltpu.HBM)
    V = pltpu.VMEM
    dma = pltpu.SemaphoreType.DMA

    def body(*refs):
        kernel(main, *refs)

    return pl.pallas_call(
        body,
        out_shape=jax.ShapeDtypeStruct((16, 2048), BF),
        in_specs=[hbm, sm, sm] + [hbm] * 9,
        out_specs=vm,
        scratch_shapes=[
            V((128, M), F32), V(depth.shape, BF), V(har.shape, BF), V(hart.shape, BF), V(harz.shape, BF), V(hartz.shape, BF),
            V(inner.shape, F32), V(outer.shape, F32), V(back.shape, BF),
            V((512, 1024), BF),
            V((1024, 1024), BF),
            V((256, 128), F32),
            V((32, 1024), F32),
            V((1024, 128), F32),
            V((1024, 1024), BF),
            V((2048, 128), F32),
            V((16, 64, 128), BF),
            V((16, 64, 128), BF),
            V((16, 64, 128), BF),
            V((16, 64, 128), BF),
            V((16, 8, 128), F32),
            V((16, 8, 128), F32),
            V((16, 8, 128), F32),
            V((16, 8, 128), F32),
            V((64, 128), F32),
            V((32, 64, 128), F32),
            V((256, 128), F32),
            V((256, 128), F32),
            V((256, 128), F32),
            V((16, 16, 128), BF),
            V((16, 16, 128), BF),
            V((256, 128), F32),
            V((128, 256), F32),
            dma((44,)), dma((32,)), dma((2,)), dma((16,)), dma((16,)), dma((16,)), dma((32,)), dma((16,)), dma((16,)),
        ],
        compiler_params=pltpu.CompilerParams(collective_id=0, has_side_effects=True),
        name="hartree",
    )(orbitals, occupations, box_offsets.T, ker, depth, har, hart, harz, hartz, inner, outer, back)


def solution(mesh):
    in_specs = (P("orb", None), P("orb"), P("orb", None), P(None, "pln", "orb"))
    out_specs = P("orb", "pln")
    return jax.shard_map(per_device, mesh=mesh, in_specs=in_specs, out_specs=out_specs, check_vma=False)
```

```python
import math

import jax
import jax.numpy as jnp
import numpy as np
from jax import lax
from jax.experimental import pallas as pl
from jax.experimental.pallas import tpu as pltpu
from jax.sharding import PartitionSpec as P

G = 128
BOX = 32
M = 256
N_ORB = 32
N_PLN = 16
BF = jnp.bfloat16
F32 = jnp.float32

MAGIC_TAPS = (
    8.433424733352934e-07,
    -1.290557201342061e-05,
    8.76298447621056e-05,
    -0.00030158038132690465,
    0.001747237136729939,
    -0.009420470302010804,
    0.023738214637249424,
    0.0612625895831208,
    0.9940415697834004,
    -0.06048952891969835,
    -0.021030251609303816,
    0.013372634148547948,
    -0.0034412814449349387,
    0.0004944322768868992,
    -5.185986881173433e-05,
    2.7273449291197967e-06,
)


FAR = sorted(
    [(a, b) for a in range(4) for b in range(4)],
    key=lambda d: -min(d[0], 4 - d[0]) - min(d[1], 4 - d[1]),
)


def split(values):
    high = np.asarray(values, np.float32).astype(BF)
    low = (np.asarray(values, np.float32) - high.astype(np.float32)).astype(BF)
    return np.stack([high, low])


def tables():
    taps = np.asarray(MAGIC_TAPS, np.float32)
    magic = np.zeros((BOX, BOX), np.float32)
    for i in range(BOX):
        for k in range(BOX):
            if -8 <= k - i <= 7:
                magic[i, k] = taps[k - i + 8]
    depth = np.repeat(magic, N_PLN, axis=1)
    angle = 2.0 * math.pi * (np.outer(np.arange(M), np.arange(G)) % M) / M
    hartley = np.cos(angle) + np.sin(angle)
    cyclic = np.arange(G).reshape(8, N_PLN).T.reshape(-1)
    inner = np.tile(magic.T, (1, BOX)).astype(np.float32)
    outer = np.repeat(magic.T, BOX, axis=1).astype(np.float32)
    back = np.concatenate([magic[:, 0::2].T, magic[:, 1::2].T])
    return split(depth), split(hartley), split(hartley.T), split(hartley[:, cyclic]), split(hartley.T[cyclic]), inner, outer, split(back), float(magic[0, 0]) ** 2


def dg(a, b, ca, cb):
    return lax.dot_general(a, b, (((ca,), (cb,)), ((), ())), preferred_element_type=F32)


def halves(a):
    high = a.astype(BF)
    return high, (a - high.astype(F32)).astype(BF)


def dot3(a, bh, bl, ca, cb):
    ah, al = halves(a)
    return dg(ah, bh, ca, cb) + (dg(al, bh, ca, cb) + dg(ah, bl, ca, cb))


def dot3r(ah, al, b, ca, cb):
    bh, bl = halves(b)
    return dg(ah, bh, ca, cb) + (dg(al, bh, ca, cb) + dg(ah, bl, ca, cb))


def kernel(
    main,
    orb_hbm, occ_ref, off_ref, ker_hbm, depth_hbm, har_hbm, hart_hbm, harz_hbm, hartz_hbm, inner_hbm, outer_hbm, back_hbm,
    out_ref,
    ker_ref, depth_ref, har_ref, hart_ref, harz_ref, hartz_ref, inner_ref, outer_ref, back_ref,
    x_s, kt_s, psq_s, own_s, q_s, oh_s, d_s, s1, r1, m1, mr1, s2, r2, s3, r3, w_s, r4, s5, r5, fs_s, s6, r6, gs_s, kp_s,
    load_sem, send_sem, rsm, rs1, rs2, rs3, rs4, rs5, rs6,
):
    o = lax.axis_index("orb")
    p = lax.axis_index("pln")
    barrier = pltpu.get_barrier_semaphore()

    def greet(axis, me, count):
        def step(d, carry):
            pl.semaphore_signal(
                barrier, inc=1, device_id={axis: lax.rem(me + d, count)}, device_id_type=pl.DeviceIdType.MESH
            )
            return carry

        lax.fori_loop(1, count, step, 0)

    greet("orb", o, N_ORB)
    greet("pln", p, N_PLN)

    pairs = (
        (depth_hbm, depth_ref), (inner_hbm, inner_ref), (outer_hbm, outer_ref), (har_hbm, har_ref),
        (ker_hbm, ker_ref), (hart_hbm, hart_ref), (back_hbm, back_ref), (harz_hbm, harz_ref), (hartz_hbm, hartz_ref),
    )
    loads = [pltpu.make_async_copy(a, b, load_sem.at[i]) for i, (a, b) in enumerate(pairs)]
    rows_of = lambda k: pltpu.make_async_copy(
        orb_hbm.at[:, pl.ds(pl.multiple_of(k * 1024, 1024), 1024)],
        x_s.at[pl.ds(pl.multiple_of(k * 16, 16), 16), :],
        load_sem.at[12 + k],
    )

    def start_rows(k, carry):
        rows_of(k).start()
        return carry

    def wait_rows(k, carry):
        rows_of(k).wait()
        return carry

    for i in (1, 2, 0):
        loads[i].start()
    lax.fori_loop(0, BOX, start_rows, 0)
    for i in range(3, 9):
        loads[i].start()
    loads[1].wait()
    loads[2].wait()

    def copy_to(axis, src, dst, recv, slot, other, sem_slot):
        return pltpu.make_async_remote_copy(
            src_ref=src, dst_ref=dst, send_sem=send_sem.at[sem_slot], recv_sem=recv.at[slot],
            device_id={axis: other}, device_id_type=pl.DeviceIdType.MESH,
        )

    def far(i):
        return lax.rem(p + 8 + (1 - 2 * lax.rem(i, 2)) * ((i + 1) // 2), N_PLN)

    def send_all(axis, me, count, src_of, dst, recv):
        def step(i, carry):
            other = far(i)
            copy_to(axis, src_of(other), dst.at[me], recv, me, other, i).start()
            return carry

        lax.fori_loop(0, count - 1, step, 0)

    def wait_all(axis, me, count, src_of, dst, recv):
        def step(i, carry):
            other = far(count - 2 - i)
            copy_to(axis, src_of(other), dst.at[other], recv, other, other, i).wait()
            return carry

        lax.fori_loop(0, count - 1, step, 0)

    col1024 = lax.broadcasted_iota(jnp.int32, (BOX, 1024), 1)
    row32 = lax.broadcasted_iota(jnp.int32, (BOX, 1024), 0)
    def reach(i):
        return max(i - 1, 0) * 256, min(i + 2, 4) * 256

    for i in range(4):
        lo, hi = reach(i)
        inner = inner_ref[:, lo:hi]
        spot = col1024[:, lo:hi] - row32[:, lo:hi]

        def make_kt(q, carry, lo=lo, hi=hi, inner=inner, spot=spot):
            block = jnp.where(spot == q * BOX, 0.0, inner * outer_ref[pl.ds(q, 1), lo:hi])
            kt_s[pl.ds(pl.multiple_of(q * BOX, BOX), BOX), lo:hi] = block.astype(BF)
            return carry

        lax.fori_loop(8 * i, 8 * i + 8, make_kt, 0)

    def filtered(a, back):
        low = a.astype(BF)
        parts = []
        for i in range(4):
            lo, hi = reach(i)
            piece = kt_s[i * 256 : i * 256 + 256, lo:hi] if back else kt_s[lo:hi, i * 256 : i * 256 + 256]
            parts.append(dg(low[:, lo:hi], piece, 1, 1 if back else 0))
        return main * a + jnp.concatenate(parts, axis=1)


    lane = lax.broadcasted_iota(jnp.int32, (8, 128), 1)
    row = lax.broadcasted_iota(jnp.int32, (BOX, BOX), 0)
    col = lax.broadcasted_iota(jnp.int32, (BOX, BOX), 1)
    first_plane = jnp.zeros((BOX, BOX), jnp.int32)
    for n in range(N_PLN):
        first_plane = jnp.where(row // 2 == n, (p - off_ref[0, n] + 128) & 15, first_plane)
    hot = jnp.where(col == first_plane + 16 * (row % 2), 1.0, 0.0).astype(BF)
    loads[0].wait()
    lane512 = lax.broadcasted_iota(jnp.int32, (BOX, 512), 1) % N_PLN
    same = lax.broadcasted_iota(jnp.int32, (BOX, 512), 0) // 2 == lane512
    eh = jnp.where(same, dg(hot, depth_ref[0], 1, 0), 0.0).astype(BF)
    el = jnp.where(same, dg(hot, depth_ref[1], 1, 0), 0.0).astype(BF)
    lax.fori_loop(0, BOX, wait_rows, 0)
    x = x_s[...]
    s = dg(jnp.concatenate([eh, el], axis=0), x, 1, 0)
    psi = filtered(s[:BOX] + s[BOX:], False)
    psi = psi * psi
    for t in range(8):
        psq_s[t * BOX : (t + 1) * BOX, :] = psi[:, t * 128 : (t + 1) * 128]

    pattern = lax.broadcasted_iota(jnp.int32, (BOX, 1024), 0)
    pattern = 4 * (pattern % 8) + pattern // 8

    def place(n, carry):
        weight = occ_ref[n]
        ox = off_ref[2, n]
        oz = off_ref[0, n]
        inside = (lane >= ox) & (lane < ox + BOX)
        plane = (oz + ((p - oz + 128) & 15) - p) >> 4
        for h in range(2):
            v = psq_s[pl.ds(n * 2 + h, 8, stride=BOX), :] * weight
            for j in range(4):
                turned = pltpu.roll(v, lax.rem(ox + 128 - 32 * j, 128), 1)
                at = pl.multiple_of(((n * 2 + h) * 4 + j) * 8, 8)
                q_s[pl.ds(at, 8), :] = jnp.where(inside, turned, 0.0)
            base = (plane + h) * G + off_ref[1, n]
            at = pl.multiple_of((n * 2 + h) * BOX, BOX)
            oh_s[pl.ds(at, BOX), :] = jnp.where(col1024 == pattern + base, 1.0, 0.0).astype(BF)
        return carry

    lax.fori_loop(0, N_PLN, place, 0)

    for i in range(3, 9):
        loads[i].wait()
    hh, hl = har_ref[0], har_ref[1]
    qh, ql = halves(q_s[...])
    both = dg(jnp.concatenate([qh, ql], axis=1), oh_s[...], 0, 0)
    planes = both[:G] + both[G:]
    d = dot3r(hh, hl, planes, 1, 0)
    for z in range(8):
        d_s[pl.ds(z, 256, stride=8), :] = d[:, z * 128 : (z + 1) * 128]

    core = lax.rem(o, 2)
    cx, cy = o // 8, lax.rem(o // 2, 4)
    mate = o + 1 - 2 * core
    here = o // 2

    def chip(step, sign):
        dx, dy = FAR[step]
        return 4 * lax.rem(cx + sign * dx + 4, 4) + lax.rem(cy + sign * dy + 4, 4)

    def block(owner):
        return d_s[pl.ds(pl.multiple_of(owner * 64, 64), 64), :]

    def to_mate(part):
        rows = pl.ds(part * 8, 8)
        return copy_to("orb", m1.at[rows], mr1.at[rows], rsm, part, mate, 30 + part)

    def to_chip(step):
        return copy_to("orb", s1.at[step], r1.at[here], rs1, here, 2 * chip(step, 1) + core, step)

    def from_chip(step):
        src = chip(step, -1)
        return copy_to("orb", s1.at[step], r1.at[src], rs1, src, 2 * src + core, step)

    for step in range(16):
        m1[step] = block(2 * chip(step, 1) + 1 - core).astype(BF)
        if step == 7:
            pl.semaphore_wait(barrier, N_ORB - 1 + N_PLN - 1)
            to_mate(0).start()
    to_mate(1).start()
    for step in range(15):
        if step % 8 == 0:
            to_mate(step // 8).wait()
        s1[step] = (block(2 * chip(step, 1) + core) + mr1[step].astype(F32)).astype(BF)
        to_chip(step).start()
    tr = block(o) + mr1[15].astype(F32)

    oz_own = off_ref[0, p]
    own_hot = jnp.where(col == ((row // 2 - oz_own + 128) & 15) + 16 * (row % 2), 1.0, 0.0).astype(BF)
    oh = jnp.where(lane512 == p, dg(own_hot, depth_ref[0], 1, 0), 0.0).astype(BF)
    ol = jnp.where(lane512 == p, dg(own_hot, depth_ref[1], 1, 0), 0.0).astype(BF)
    back_h = dg(back_ref[0], own_hot, 1, 1).astype(BF)
    back_l = dg(back_ref[1], own_hot, 1, 1).astype(BF)
    s_own = dg(jnp.concatenate([oh, ol], axis=0), x_s[...], 1, 0)
    own_s[...] = filtered(s_own[:BOX] + s_own[BOX:], False)

    for h in range(2):
        d_s[h * 128 : (h + 1) * 128, :] = ker_ref[:, h * 128 : (h + 1) * 128] * (1.0 / float(M) ** 3)
    for kx in range(8):
        for h in range(2):
            kp_s[kx * 16 : (kx + 1) * 16, h * 128 : (h + 1) * 128] = d_s[pl.ds(h * 128 + kx, 16, stride=8), :]

    for step in reversed(range(15)):
        from_chip(step).wait()
        tr = tr + r1[chip(step, -1)].astype(F32)

    y = dot3(tr, hh, hl, 1, 1)
    for i in range(N_PLN):
        total = jnp.zeros((8, 128), F32)
        for kx in range(8):
            v = y[kx * 8 : (kx + 1) * 8, (i // 8) * 128 : (i // 8) * 128 + 128]
            shift = 16 * (kx - i % 8) % 128
            v = pltpu.roll(v, shift, 1) if shift else v
            total = jnp.where(lane // 16 == kx, v, total)
        s2[i] = total.astype(BF)
    send_all("pln", p, N_PLN, lambda i: s2.at[i], r2, rs2)
    r2[p] = s2[p]
    wait_all("pln", p, N_PLN, lambda i: s2.at[i], r2, rs2)

    grid_z = r2[...].astype(F32).reshape(G, 128)
    spectrum = dot3(grid_z.T, harz_ref[0], harz_ref[1], 1, 1)
    spectrum = spectrum * kp_s[...]
    back_z = dot3r(hartz_ref[0], hartz_ref[1], spectrum, 1, 1)
    s3[...] = back_z.reshape(N_PLN, 8, 128)
    send_all("pln", p, N_PLN, lambda i: s3.at[i], r3, rs3)
    r3[p] = s3[p]
    wait_all("pln", p, N_PLN, lambda i: s3.at[i], r3, rs3)

    blocks = []
    for kx in range(8):
        sides = []
        for h in range(2):
            total = jnp.zeros((8, 128), F32)
            for i in range(8):
                v = r3[h * 8 + i]
                shift = 16 * (i - kx) % 128
                v = pltpu.roll(v, shift, 1) if shift else v
                total = jnp.where(lane // 16 == i, v, total)
            sides.append(total)
        blocks.append(jnp.concatenate(sides, axis=1))
    w_s[...] = dot3(jnp.concatenate(blocks, axis=0), hh, hl, 1, 0)
    def rows64(i):
        return pl.ds(pl.multiple_of(i * 64, 64), 64)

    def gather(step):
        return copy_to("orb", w_s, r4.at[rows64(o)], rs4, o, 2 * chip(step, 1) + core, step)

    def arrive(step):
        src = 2 * chip(step, -1) + core
        return copy_to("orb", w_s, r4.at[rows64(src)], rs4, src, src, step)

    def forward(step):
        src = 2 * chip(step, -1) + core
        return copy_to("orb", r4.at[rows64(src)], r4.at[rows64(src)], rs4, src, mate, step + 16)

    def passed(step):
        src = 2 * chip(step, -1) + 1 - core
        return copy_to("orb", w_s, r4.at[rows64(src)], rs4, src, mate, step + 16)

    first = copy_to("orb", w_s, r4.at[rows64(o)], rs4, o, mate, 15)
    for step in range(15):
        gather(step).start()
    first.start()
    r4[rows64(o), :] = w_s[...]
    for step in reversed(range(15)):
        arrive(step).wait_recv()
        forward(step).start()
    for step in range(15):
        gather(step).wait_send()
    first.wait_send()
    for step in reversed(range(16)):
        passed(step).wait_recv()
        if step < 15:
            forward(step).wait_send()


    w = jnp.concatenate([r4[pl.ds(z, 256, stride=8), :] for z in range(8)], axis=1)
    v = dot3r(hart_ref[0], hart_ref[1], w, 1, 0)
    vh, vl = halves(v)
    both = dg(oh_s[...], jnp.concatenate([vh, vl], axis=0), 1, 1)
    q_s[...] = both[:, :G] + both[:, G:]

    def rows16(i):
        return pl.ds(pl.multiple_of(i * 16, 16), 16)

    def send_box(i):
        n = far(i)
        return copy_to("pln", s5.at[rows16(n)], r5.at[rows16(p)], rs5, p, n, i)

    def wait_box(i, carry):
        n = far(N_PLN - 2 - i)
        copy_to("pln", s5.at[rows16(n)], r5.at[rows16(n)], rs5, n, n, i).wait()
        return carry

    def box(n, put):
        ox = off_ref[2, n]
        for h in range(2):
            total = jnp.zeros((8, 128), F32)
            for j in range(4):
                u = q_s[pl.ds(pl.multiple_of(((n * 2 + h) * 4 + j) * 8, 8), 8), :]
                u = pltpu.roll(u, lax.rem(128 + 32 * j - ox, 128), 1)
                total = jnp.where(lane // 32 == j, u, total)
            put[pl.ds(pl.multiple_of(n * 16 + h * 8, 8), 8), :] = total

    def box_out(i, carry):
        box(far(i), s5)
        send_box(i).start()
        return carry

    lax.fori_loop(0, N_PLN - 1, box_out, 0)
    box(p, r5)
    lax.fori_loop(0, N_PLN - 1, wait_box, 0)

    own = own_s[...]
    u = jnp.concatenate(
        [r5[pl.ds(t, BOX, stride=8), :] * own[:, t * 128 : (t + 1) * 128] for t in range(8)], axis=1
    )
    u = filtered(u, True)
    f = dot3r(back_h, back_l, u, 1, 0)
    for t in range(16):
        part = f[(t // 8) * 16 : (t // 8) * 16 + 16, (t % 8) * 128 : (t % 8) * 128 + 128]
        fs_s[t * 16 : (t + 1) * 16, :] = part
    for i in range(N_PLN):
        s6[i] = fs_s[pl.ds(i, 16, stride=16), :].astype(BF)
    send_all("pln", p, N_PLN, lambda i: s6.at[i], r6, rs6)
    r6[p] = s6[p]
    wait_all("pln", p, N_PLN, lambda i: s6.at[i], r6, rs6)
    gs_s[...] = r6[...].astype(F32).reshape(256, 128)
    for t in range(16):
        out_ref[:, t * 128 : (t + 1) * 128] = gs_s[pl.ds(t, 16, stride=16), :].astype(BF)


def per_device(orbitals, occupations, box_offsets, kernel_spectrum):
    depth, har, hart, harz, hartz, inner, outer, back, main = tables()
    ker = kernel_spectrum.transpose(1, 2, 0).reshape(128, M)
    vm = pl.BlockSpec(memory_space=pltpu.VMEM)
    sm = pl.BlockSpec(memory_space=pltpu.SMEM)
    hbm = pl.BlockSpec(memory_space=pltpu.HBM)
    V = pltpu.VMEM
    dma = pltpu.SemaphoreType.DMA

    def body(*refs):
        kernel(main, *refs)

    return pl.pallas_call(
        body,
        out_shape=pltpu.VMEM((16, 2048), BF),
        in_specs=[hbm, sm, sm] + [hbm] * 9,
        out_specs=vm,
        scratch_shapes=[
            V((128, M), F32), V(depth.shape, BF), V(har.shape, BF), V(hart.shape, BF), V(harz.shape, BF), V(hartz.shape, BF),
            V(inner.shape, F32), V(outer.shape, F32), V(back.shape, BF),
            V((512, 1024), BF),
            V((1024, 1024), BF),
            V((256, 128), F32),
            V((32, 1024), F32),
            V((1024, 128), F32),
            V((1024, 1024), BF),
            V((2048, 128), F32),
            V((16, 64, 128), BF),
            V((16, 64, 128), BF),
            V((16, 64, 128), BF),
            V((16, 64, 128), BF),
            V((16, 8, 128), BF),
            V((16, 8, 128), BF),
            V((16, 8, 128), F32),
            V((16, 8, 128), F32),
            V((64, 128), F32),
            V((2048, 128), F32),
            V((256, 128), F32),
            V((256, 128), F32),
            V((256, 128), F32),
            V((16, 16, 128), BF),
            V((16, 16, 128), BF),
            V((256, 128), F32),
            V((128, 256), F32),
            dma((44,)), dma((32,)), dma((2,)), dma((16,)), dma((16,)), dma((16,)), dma((32,)), dma((16,)), dma((16,)),
        ],
        compiler_params=pltpu.CompilerParams(collective_id=0, has_side_effects=True),
        name="hartree",
    )(orbitals, occupations, box_offsets.T, ker, depth, har, hart, harz, hartz, inner, outer, back)


def solution(mesh):
    in_specs = (P("orb", None), P("orb"), P("orb", None), P(None, "pln", "orb"))
    out_specs = P("orb", "pln")
    return jax.shard_map(per_device, mesh=mesh, in_specs=in_specs, out_specs=out_specs, check_vma=False)
```

```python
import math

import jax
import jax.numpy as jnp
import numpy as np
from jax import lax
from jax.experimental import pallas as pl
from jax.experimental.pallas import tpu as pltpu
from jax.sharding import PartitionSpec as P

G = 128
BOX = 32
M = 256
N_ORB = 32
N_PLN = 16
BF = jnp.bfloat16
F32 = jnp.float32

MAGIC_TAPS = (
    8.433424733352934e-07,
    -1.290557201342061e-05,
    8.76298447621056e-05,
    -0.00030158038132690465,
    0.001747237136729939,
    -0.009420470302010804,
    0.023738214637249424,
    0.0612625895831208,
    0.9940415697834004,
    -0.06048952891969835,
    -0.021030251609303816,
    0.013372634148547948,
    -0.0034412814449349387,
    0.0004944322768868992,
    -5.185986881173433e-05,
    2.7273449291197967e-06,
)


FAR = sorted(
    [(a, b) for a in range(4) for b in range(4)],
    key=lambda d: -min(d[0], 4 - d[0]) - min(d[1], 4 - d[1]),
)


def split(values):
    high = np.asarray(values, np.float32).astype(BF)
    low = (np.asarray(values, np.float32) - high.astype(np.float32)).astype(BF)
    return np.stack([high, low])


def tables():
    taps = np.asarray(MAGIC_TAPS, np.float32)
    magic = np.zeros((BOX, BOX), np.float32)
    for i in range(BOX):
        for k in range(BOX):
            if -8 <= k - i <= 7:
                magic[i, k] = taps[k - i + 8]
    depth = np.repeat(magic, N_PLN, axis=1)
    angle = 2.0 * math.pi * (np.outer(np.arange(M), np.arange(G)) % M) / M
    hartley = np.cos(angle) + np.sin(angle)
    cyclic = np.arange(G).reshape(8, N_PLN).T.reshape(-1)
    inner = np.tile(magic.T, (1, BOX)).astype(np.float32)
    outer = np.repeat(magic.T, BOX, axis=1).astype(np.float32)
    back = np.concatenate([magic[:, 0::2].T, magic[:, 1::2].T])
    return split(depth), split(hartley), split(hartley.T), split(hartley[:, cyclic]), split(hartley.T[cyclic]), inner, outer, split(back), float(magic[0, 0]) ** 2


def dg(a, b, ca, cb):
    return lax.dot_general(a, b, (((ca,), (cb,)), ((), ())), preferred_element_type=F32)


def halves(a):
    high = a.astype(BF)
    return high, (a - high.astype(F32)).astype(BF)


def dot3(a, bh, bl, ca, cb):
    ah, al = halves(a)
    return dg(ah, bh, ca, cb) + (dg(al, bh, ca, cb) + dg(ah, bl, ca, cb))


def dot3r(ah, al, b, ca, cb):
    bh, bl = halves(b)
    return dg(ah, bh, ca, cb) + (dg(al, bh, ca, cb) + dg(ah, bl, ca, cb))


def kernel(
    main,
    orb_hbm, occ_ref, off_ref, ker_hbm, depth_hbm, har_hbm, hart_hbm, harz_hbm, hartz_hbm, inner_hbm, outer_hbm, back_hbm,
    out_ref,
    ker_ref, depth_ref, har_ref, hart_ref, harz_ref, hartz_ref, inner_ref, outer_ref, back_ref,
    x_s, kt_s, psq_s, own_s, q_s, oh_s, d_s, s1, r1, m1, mr1, s2, r2, s3, r3, w_s, l_s, rl, r4, s5, r5, fs_s, s6, r6, gs_s, kp_s,
    load_sem, send_sem, rsm, rs1, rs2, rs3, rs4, rsl, rs5, rs6,
):
    o = lax.axis_index("orb")
    p = lax.axis_index("pln")
    barrier = pltpu.get_barrier_semaphore()

    def greet(axis, me, count):
        def step(d, carry):
            pl.semaphore_signal(
                barrier, inc=1, device_id={axis: lax.rem(me + d, count)}, device_id_type=pl.DeviceIdType.MESH
            )
            return carry

        lax.fori_loop(1, count, step, 0)

    greet("orb", o, N_ORB)
    greet("pln", p, N_PLN)

    pairs = (
        (depth_hbm, depth_ref), (inner_hbm, inner_ref), (outer_hbm, outer_ref), (har_hbm, har_ref),
        (ker_hbm, ker_ref), (hart_hbm, hart_ref), (back_hbm, back_ref), (harz_hbm, harz_ref), (hartz_hbm, hartz_ref),
    )
    loads = [pltpu.make_async_copy(a, b, load_sem.at[i]) for i, (a, b) in enumerate(pairs)]
    rows_of = lambda k: pltpu.make_async_copy(
        orb_hbm.at[:, pl.ds(pl.multiple_of(k * 1024, 1024), 1024)],
        x_s.at[pl.ds(pl.multiple_of(k * 16, 16), 16), :],
        load_sem.at[12 + k],
    )

    def start_rows(k, carry):
        rows_of(k).start()
        return carry

    def wait_rows(k, carry):
        rows_of(k).wait()
        return carry

    for i in (1, 2, 0):
        loads[i].start()
    lax.fori_loop(0, BOX, start_rows, 0)
    for i in range(3, 9):
        loads[i].start()
    loads[1].wait()
    loads[2].wait()

    def copy_to(axis, src, dst, recv, slot, other, sem_slot):
        return pltpu.make_async_remote_copy(
            src_ref=src, dst_ref=dst, send_sem=send_sem.at[sem_slot], recv_sem=recv.at[slot],
            device_id={axis: other}, device_id_type=pl.DeviceIdType.MESH,
        )

    def far(i):
        return lax.rem(p + 8 + (1 - 2 * lax.rem(i, 2)) * ((i + 1) // 2), N_PLN)

    def send_all(axis, me, count, src_of, dst, recv):
        def step(i, carry):
            other = far(i)
            copy_to(axis, src_of(other), dst.at[me], recv, me, other, i).start()
            return carry

        lax.fori_loop(0, count - 1, step, 0)

    def wait_all(axis, me, count, src_of, dst, recv):
        def step(i, carry):
            other = far(count - 2 - i)
            copy_to(axis, src_of(other), dst.at[other], recv, other, other, i).wait()
            return carry

        lax.fori_loop(0, count - 1, step, 0)

    col1024 = lax.broadcasted_iota(jnp.int32, (BOX, 1024), 1)
    row32 = lax.broadcasted_iota(jnp.int32, (BOX, 1024), 0)
    def reach(i):
        return max(i - 1, 0) * 256, min(i + 2, 4) * 256

    for i in range(4):
        lo, hi = reach(i)
        inner = inner_ref[:, lo:hi]
        spot = col1024[:, lo:hi] - row32[:, lo:hi]

        def make_kt(q, carry, lo=lo, hi=hi, inner=inner, spot=spot):
            block = jnp.where(spot == q * BOX, 0.0, inner * outer_ref[pl.ds(q, 1), lo:hi])
            kt_s[pl.ds(pl.multiple_of(q * BOX, BOX), BOX), lo:hi] = block.astype(BF)
            return carry

        lax.fori_loop(8 * i, 8 * i + 8, make_kt, 0)

    def filtered(a, back):
        low = a.astype(BF)
        parts = []
        for i in range(4):
            lo, hi = reach(i)
            piece = kt_s[i * 256 : i * 256 + 256, lo:hi] if back else kt_s[lo:hi, i * 256 : i * 256 + 256]
            parts.append(dg(low[:, lo:hi], piece, 1, 1 if back else 0))
        return main * a + jnp.concatenate(parts, axis=1)


    lane = lax.broadcasted_iota(jnp.int32, (8, 128), 1)
    row = lax.broadcasted_iota(jnp.int32, (BOX, BOX), 0)
    col = lax.broadcasted_iota(jnp.int32, (BOX, BOX), 1)
    first_plane = jnp.zeros((BOX, BOX), jnp.int32)
    for n in range(N_PLN):
        first_plane = jnp.where(row // 2 == n, (p - off_ref[0, n] + 128) & 15, first_plane)
    hot = jnp.where(col == first_plane + 16 * (row % 2), 1.0, 0.0).astype(BF)
    loads[0].wait()
    lane512 = lax.broadcasted_iota(jnp.int32, (BOX, 512), 1) % N_PLN
    same = lax.broadcasted_iota(jnp.int32, (BOX, 512), 0) // 2 == lane512
    eh = jnp.where(same, dg(hot, depth_ref[0], 1, 0), 0.0).astype(BF)
    el = jnp.where(same, dg(hot, depth_ref[1], 1, 0), 0.0).astype(BF)
    lax.fori_loop(0, BOX, wait_rows, 0)
    x = x_s[...]
    s = dg(jnp.concatenate([eh, el], axis=0), x, 1, 0)
    psi = filtered(s[:BOX] + s[BOX:], False)
    psi = psi * psi
    for t in range(8):
        psq_s[t * BOX : (t + 1) * BOX, :] = psi[:, t * 128 : (t + 1) * 128]

    pattern = lax.broadcasted_iota(jnp.int32, (BOX, 1024), 0)
    pattern = 4 * (pattern % 8) + pattern // 8

    def place(n, carry):
        weight = occ_ref[n]
        ox = off_ref[2, n]
        oz = off_ref[0, n]
        inside = (lane >= ox) & (lane < ox + BOX)
        plane = (oz + ((p - oz + 128) & 15) - p) >> 4
        for h in range(2):
            v = psq_s[pl.ds(n * 2 + h, 8, stride=BOX), :] * weight
            for j in range(4):
                turned = pltpu.roll(v, lax.rem(ox + 128 - 32 * j, 128), 1)
                at = pl.multiple_of(((n * 2 + h) * 4 + j) * 8, 8)
                q_s[pl.ds(at, 8), :] = jnp.where(inside, turned, 0.0)
            base = (plane + h) * G + off_ref[1, n]
            at = pl.multiple_of((n * 2 + h) * BOX, BOX)
            oh_s[pl.ds(at, BOX), :] = jnp.where(col1024 == pattern + base, 1.0, 0.0).astype(BF)
        return carry

    lax.fori_loop(0, N_PLN, place, 0)

    for i in range(3, 9):
        loads[i].wait()
    hh, hl = har_ref[0], har_ref[1]
    qh, ql = halves(q_s[...])
    both = dg(jnp.concatenate([qh, ql], axis=1), oh_s[...], 0, 0)
    planes = both[:G] + both[G:]
    d = dot3r(hh, hl, planes, 1, 0)
    for z in range(8):
        d_s[pl.ds(z, 256, stride=8), :] = d[:, z * 128 : (z + 1) * 128]

    core = lax.rem(o, 2)
    cx, cy = o // 8, lax.rem(o // 2, 4)
    mate = o + 1 - 2 * core
    here = o // 2

    def chip(step, sign):
        dx, dy = FAR[step]
        return 4 * lax.rem(cx + sign * dx + 4, 4) + lax.rem(cy + sign * dy + 4, 4)

    def block(owner):
        return d_s[pl.ds(pl.multiple_of(owner * 64, 64), 64), :]

    def to_mate(part):
        rows = pl.ds(part * 8, 8)
        return copy_to("orb", m1.at[rows], mr1.at[rows], rsm, part, mate, 30 + part)

    def to_chip(step):
        return copy_to("orb", s1.at[step], r1.at[here], rs1, here, 2 * chip(step, 1) + core, step)

    def from_chip(step):
        src = chip(step, -1)
        return copy_to("orb", s1.at[step], r1.at[src], rs1, src, 2 * src + core, step)

    for step in range(16):
        m1[step] = block(2 * chip(step, 1) + 1 - core).astype(BF)
        if step == 7:
            pl.semaphore_wait(barrier, N_ORB - 1 + N_PLN - 1)
            to_mate(0).start()
    to_mate(1).start()
    for step in range(15):
        if step % 8 == 0:
            to_mate(step // 8).wait()
        s1[step] = (block(2 * chip(step, 1) + core) + mr1[step].astype(F32)).astype(BF)
        to_chip(step).start()
    tr = block(o) + mr1[15].astype(F32)

    oz_own = off_ref[0, p]
    own_hot = jnp.where(col == ((row // 2 - oz_own + 128) & 15) + 16 * (row % 2), 1.0, 0.0).astype(BF)
    oh = jnp.where(lane512 == p, dg(own_hot, depth_ref[0], 1, 0), 0.0).astype(BF)
    ol = jnp.where(lane512 == p, dg(own_hot, depth_ref[1], 1, 0), 0.0).astype(BF)
    back_h = dg(back_ref[0], own_hot, 1, 1).astype(BF)
    back_l = dg(back_ref[1], own_hot, 1, 1).astype(BF)
    s_own = dg(jnp.concatenate([oh, ol], axis=0), x_s[...], 1, 0)
    own_s[...] = filtered(s_own[:BOX] + s_own[BOX:], False)

    for h in range(2):
        d_s[h * 128 : (h + 1) * 128, :] = ker_ref[:, h * 128 : (h + 1) * 128] * (1.0 / float(M) ** 3)
    for kx in range(8):
        for h in range(2):
            kp_s[kx * 16 : (kx + 1) * 16, h * 128 : (h + 1) * 128] = d_s[pl.ds(h * 128 + kx, 16, stride=8), :]

    for step in reversed(range(15)):
        from_chip(step).wait()
        tr = tr + r1[chip(step, -1)].astype(F32)

    y = dot3(tr, hh, hl, 1, 1)
    for i in range(N_PLN):
        total = jnp.zeros((8, 128), F32)
        for kx in range(8):
            v = y[kx * 8 : (kx + 1) * 8, (i // 8) * 128 : (i // 8) * 128 + 128]
            shift = 16 * (kx - i % 8) % 128
            v = pltpu.roll(v, shift, 1) if shift else v
            total = jnp.where(lane // 16 == kx, v, total)
        s2[i] = total.astype(BF)
    send_all("pln", p, N_PLN, lambda i: s2.at[i], r2, rs2)
    r2[p] = s2[p]
    wait_all("pln", p, N_PLN, lambda i: s2.at[i], r2, rs2)

    grid_z = r2[...].astype(F32).reshape(G, 128)
    spectrum = dot3(grid_z.T, harz_ref[0], harz_ref[1], 1, 1)
    spectrum = spectrum * kp_s[...]
    back_z = dot3r(hartz_ref[0], hartz_ref[1], spectrum, 1, 1)
    s3[...] = back_z.reshape(N_PLN, 8, 128)
    send_all("pln", p, N_PLN, lambda i: s3.at[i], r3, rs3)
    r3[p] = s3[p]
    wait_all("pln", p, N_PLN, lambda i: s3.at[i], r3, rs3)

    blocks = []
    for kx in range(8):
        sides = []
        for h in range(2):
            total = jnp.zeros((8, 128), F32)
            for i in range(8):
                v = r3[h * 8 + i]
                shift = 16 * (i - kx) % 128
                v = pltpu.roll(v, shift, 1) if shift else v
                total = jnp.where(lane // 16 == i, v, total)
            sides.append(total)
        blocks.append(jnp.concatenate(sides, axis=1))
    w_high, w_low = halves(dot3(jnp.concatenate(blocks, axis=0), hh, hl, 1, 0))
    w_s[...] = w_high
    l_s[...] = w_low
    def rows64(i):
        return pl.ds(pl.multiple_of(i * 64, 64), 64)

    def gather(step):
        return copy_to("orb", w_s, r4.at[rows64(o)], rs4, o, 2 * chip(step, 1) + core, step)

    def arrive(step):
        src = 2 * chip(step, -1) + core
        return copy_to("orb", w_s, r4.at[rows64(src)], rs4, src, src, step)

    def forward(step):
        src = 2 * chip(step, -1) + core
        return copy_to("orb", r4.at[rows64(src)], r4.at[rows64(src)], rs4, src, mate, step + 16)

    def passed(step):
        src = 2 * chip(step, -1) + 1 - core
        return copy_to("orb", w_s, r4.at[rows64(src)], rs4, src, mate, step + 16)

    def low_out(step):
        return copy_to("orb", l_s, rl.at[core], rsl, core, 2 * chip(step, 1) + core, step + 32)

    def low_on(src_ref):
        return copy_to("orb", src_ref, rl.at[core], rsl, core, mate, 47)

    first = copy_to("orb", w_s, r4.at[rows64(o)], rs4, o, mate, 15)
    lowest = o == 31 * core

    @pl.when(lowest)
    def _():
        for step in range(15):
            low_out(step).start()
        low_on(l_s).start()
        rl[core] = l_s[...]

    for step in range(15):
        gather(step).start()
    first.start()
    r4[rows64(o), :] = w_s[...]
    for step in reversed(range(15)):
        arrive(step).wait_recv()
        forward(step).start()

    @pl.when(jnp.logical_not(lowest))
    def _():
        low_out(0).wait_recv()
        low_on(rl.at[core]).start()

    for step in range(15):
        gather(step).wait_send()
    first.wait_send()
    for step in reversed(range(16)):
        passed(step).wait_recv()
        if step < 15:
            forward(step).wait_send()

    @pl.when(lowest)
    def _():
        for step in range(15):
            low_out(step).wait_send()

    low_on(l_s).wait_send()
    copy_to("orb", l_s, rl.at[1 - core], rsl, 1 - core, mate, 47).wait_recv()


    d_s[...] = r4[...].astype(F32)
    for i in range(2):
        d_s[i * 1984 : i * 1984 + 64, :] = d_s[i * 1984 : i * 1984 + 64, :] + rl[i].astype(F32)
    w = jnp.concatenate([d_s[pl.ds(z, 256, stride=8), :] for z in range(8)], axis=1)
    v = dot3r(hart_ref[0], hart_ref[1], w, 1, 0)
    vh, vl = halves(v)
    both = dg(oh_s[...], jnp.concatenate([vh, vl], axis=0), 1, 1)
    q_s[...] = both[:, :G] + both[:, G:]

    def rows16(i):
        return pl.ds(pl.multiple_of(i * 16, 16), 16)

    def send_box(i):
        n = far(i)
        return copy_to("pln", s5.at[rows16(n)], r5.at[rows16(p)], rs5, p, n, i)

    def wait_box(i, carry):
        n = far(N_PLN - 2 - i)
        copy_to("pln", s5.at[rows16(n)], r5.at[rows16(n)], rs5, n, n, i).wait()
        return carry

    def box(n, put):
        ox = off_ref[2, n]
        for h in range(2):
            total = jnp.zeros((8, 128), F32)
            for j in range(4):
                u = q_s[pl.ds(pl.multiple_of(((n * 2 + h) * 4 + j) * 8, 8), 8), :]
                u = pltpu.roll(u, lax.rem(128 + 32 * j - ox, 128), 1)
                total = jnp.where(lane // 32 == j, u, total)
            put[pl.ds(pl.multiple_of(n * 16 + h * 8, 8), 8), :] = total

    def box_out(i, carry):
        box(far(i), s5)
        send_box(i).start()
        return carry

    lax.fori_loop(0, N_PLN - 1, box_out, 0)
    box(p, r5)
    lax.fori_loop(0, N_PLN - 1, wait_box, 0)

    own = own_s[...]
    u = jnp.concatenate(
        [r5[pl.ds(t, BOX, stride=8), :] * own[:, t * 128 : (t + 1) * 128] for t in range(8)], axis=1
    )
    u = filtered(u, True)
    f = dot3r(back_h, back_l, u, 1, 0)
    for t in range(16):
        part = f[(t // 8) * 16 : (t // 8) * 16 + 16, (t % 8) * 128 : (t % 8) * 128 + 128]
        fs_s[t * 16 : (t + 1) * 16, :] = part
    for i in range(N_PLN):
        s6[i] = fs_s[pl.ds(i, 16, stride=16), :].astype(BF)
    send_all("pln", p, N_PLN, lambda i: s6.at[i], r6, rs6)
    r6[p] = s6[p]
    wait_all("pln", p, N_PLN, lambda i: s6.at[i], r6, rs6)
    gs_s[...] = r6[...].astype(F32).reshape(256, 128)
    for t in range(16):
        out_ref[:, t * 128 : (t + 1) * 128] = gs_s[pl.ds(t, 16, stride=16), :].astype(BF)


def per_device(orbitals, occupations, box_offsets, kernel_spectrum):
    depth, har, hart, harz, hartz, inner, outer, back, main = tables()
    ker = kernel_spectrum.transpose(1, 2, 0).reshape(128, M)
    vm = pl.BlockSpec(memory_space=pltpu.VMEM)
    sm = pl.BlockSpec(memory_space=pltpu.SMEM)
    hbm = pl.BlockSpec(memory_space=pltpu.HBM)
    V = pltpu.VMEM
    dma = pltpu.SemaphoreType.DMA

    def body(*refs):
        kernel(main, *refs)

    return pl.pallas_call(
        body,
        out_shape=pltpu.VMEM((16, 2048), BF),
        in_specs=[hbm, sm, sm] + [hbm] * 9,
        out_specs=vm,
        scratch_shapes=[
            V((128, M), F32), V(depth.shape, BF), V(har.shape, BF), V(hart.shape, BF), V(harz.shape, BF), V(hartz.shape, BF),
            V(inner.shape, F32), V(outer.shape, F32), V(back.shape, BF),
            V((512, 1024), BF),
            V((1024, 1024), BF),
            V((256, 128), F32),
            V((32, 1024), F32),
            V((1024, 128), F32),
            V((1024, 1024), BF),
            V((2048, 128), F32),
            V((16, 64, 128), BF),
            V((16, 64, 128), BF),
            V((16, 64, 128), BF),
            V((16, 64, 128), BF),
            V((16, 8, 128), BF),
            V((16, 8, 128), BF),
            V((16, 8, 128), F32),
            V((16, 8, 128), F32),
            V((64, 128), BF),
            V((64, 128), BF),
            V((2, 64, 128), BF),
            V((2048, 128), BF),
            V((256, 128), F32),
            V((256, 128), F32),
            V((256, 128), F32),
            V((16, 16, 128), BF),
            V((16, 16, 128), BF),
            V((256, 128), F32),
            V((128, 256), F32),
            dma((44,)), dma((48,)), dma((2,)), dma((16,)), dma((16,)), dma((16,)), dma((32,)), dma((2,)), dma((16,)), dma((16,)),
        ],
        compiler_params=pltpu.CompilerParams(collective_id=0, has_side_effects=True),
        name="hartree",
    )(orbitals, occupations, box_offsets.T, ker, depth, har, hart, harz, hartz, inner, outer, back)


def solution(mesh):
    in_specs = (P("orb", None), P("orb"), P("orb", None), P(None, "pln", "orb"))
    out_specs = P("orb", "pln")
    return jax.shard_map(per_device, mesh=mesh, in_specs=in_specs, out_specs=out_specs, check_vma=False)
```
